256 devices in a mesh: patch: 64 (over y, z, core), mem: 4 (over x).
Axes of the slice: x: 4, y: 4, z: 8, core: 2. Of those that a mesh axis runs over, the one named last changes fastest.
Arguments:
- atmos: bfloat16 [128, 8, 65536], P('mem', None, 'patch'), may hold values from -6 to 6
- land: bfloat16 [128, 8, 262144], P('mem', None, 'patch'), may hold values from -6 to 6
- land_mask: int32 [262144], P('patch'), may hold values 0 or 1
- tile_owner: int32 [262144, 1], P('patch'), may hold values from 0 to 63; in each aligned block of 4096 rows (0 to 4095, 4096 to 8191, ...) at most 128 rows name the same one
- tile_column: int32 [262144], P('patch'), may hold values from 0 to 1023
- tile_weight: bfloat16 [262144], P('patch'), may hold values from 0.19921875 to 1
- obs_value: float32 [32768], P('patch'), may hold values from -12 to 12
- observation_column: int32 [32768], P('patch'), may hold values from 0 to 1023
- obs_error: float32 [32768], P('patch'), may hold values from 0.5 to 4
- loc_blocks: int32 [64, 4], P('patch'), may hold values from 0 to 63, as said below
Outputs:
- atmos_analysis: bfloat16 [128, 8, 65536], P('mem', None, 'patch')
- land_analysis: bfloat16 [128, 8, 262144], P('mem', None, 'patch')
The draws below stay inside these ranges and needn't reach their ends.
Inputs may be any that keep to these rules, and one draw needn't show every extreme that they name: `tile_owner`: among the tiles of one tile block at most 128 have the same owner, and in some blocks exactly 128 do. `loc_blocks`: patches lie row by row on a grid 8 patches wide, indices taken modulo the number of patches. Row p begins with p and then names three different ones of its four grid neighbours p - 1, p + 1, p - 8, p + 8, in that order.
All inputs are finite; a program needn't handle non-finite values. No bound on the sum of `land_mask` on one device may be relied on, other than what follows from the above.
Results may differ from the reference program's by a relative error of at most 0.006.
Values may be sent and summed in bfloat16 or wider, within the bound.
No kernel may reach another device: no remote copies, remote signals or barrier semaphores. Data moves between devices by JAX's collectives and lax.ppermute only.
A program may use at most 128 MiB of HBM per device.

```python
import math
import jax
import jax.numpy as jnp
import numpy as np
from jax import lax

ENSEMBLE_COUNT = 128
LEVELS = 8
LAYERS = 8
COL_DEV = 1024
TILE_DEV = 4096
PATCH_OBS_COUNT = 512
SWEEPS = 10
NCOL = 65536
NTILE = 262144
NOBS = 32768
CAP = 128
N_PATCH = 64


def draw_loc_blocks(key, part):
    npatch = N_PATCH
    row_width = max(2, npatch // 8)
    indices = jnp.arange(npatch, dtype=jnp.int32)
    candidates = jnp.stack([indices - 1, indices + 1, indices - row_width, indices + row_width], axis=1) % npatch
    dropped = jax.random.randint(key, (npatch,), 0, 4, dtype=jnp.int32)
    places = jnp.arange(3, dtype=jnp.int32)[None, :]
    picks = (places + (places >= dropped[:, None]).astype(jnp.int32)).astype(jnp.int32)
    chosen = jnp.take_along_axis(candidates, picks, axis=1).astype(jnp.int32)
    return jnp.concatenate([indices[:, None], chosen], axis=1).astype(jnp.int32)


def set_ends(values, stream_key, smallest, largest):
    index_at = [jax.random.randint(jax.random.fold_in(stream_key, axis), (), 0, length) for axis, length in enumerate(values.shape)]
    longest = values.shape.index(max(values.shape))
    beside = index_at[:longest] + [(index_at[longest] + 1) % values.shape[longest]] + index_at[longest + 1:]
    return values.at[tuple(index_at)].set(smallest).at[tuple(beside)].set(largest)


def block_scale(key, dims, pieces, low, high):
    level, own = 1.0, jax.random.fold_in(key, 6)
    for position, parts in pieces:
        steps = jnp.exp(jax.random.uniform(jax.random.fold_in(own, position), (parts,), jnp.float32, low / len(pieces), high / len(pieces)))
        level = level * jnp.repeat(steps, dims[position] // parts).reshape([-1 if axis == position else 1 for axis in range(len(dims))])
    return level


def assign_block(key, own, number, rows, count, top, bound, lean):
    sequence = jax.random.permutation(key, count)
    packed, usual = load_shares(count, rows * top, bound, lean, True), load_shares(count, rows * top, bound, lean, False)
    places = jnp.arange(count)

    def named(sizes, turn):
        used = int((sizes > 0).sum())
        fixed = max(1, used // 4)
        shifted = fixed + (places - fixed + turn * (used - fixed)) % max(1, count - fixed)
        return jnp.zeros((count,), jnp.int32).at[sequence[jnp.where(places < fixed, places, shifted)]].set(jnp.asarray(sizes, jnp.int32))

    sizes = jnp.where(number % 4 == 0, named(packed, number // 4), named(usual, number - number // 4 - 1))
    mixed = jax.random.permutation(jax.random.fold_in(own, 3), count)
    donor, receiver = mixed[0:count // 2 * 2:2], mixed[1:count // 2 * 2:2]
    slack = jnp.minimum(sizes[donor] - 1, bound - sizes[receiver]) // 2
    slack = jnp.where((donor == sequence[0]) | (receiver == sequence[0]) | (sizes[receiver] == 0), 0, jnp.maximum(slack, 0))
    shifted = jax.random.randint(jax.random.fold_in(own, 4), (count // 2,), 0, 1 << 20) % (slack + 1)
    sizes = sizes.at[donor].add(-shifted).at[receiver].add(shifted)
    labels = jnp.searchsorted(jnp.cumsum(sizes), jnp.arange(rows * top), side="right").astype(jnp.int32)
    table = labels.reshape(top, rows).T
    table = table[jax.random.permutation(jax.random.fold_in(own, 1), rows)]
    turn = jax.random.randint(jax.random.fold_in(own, 2), (rows, 1), 0, top)
    return jnp.take_along_axis(table, (jnp.arange(top)[None, :] + turn) % top, axis=1)


def load_shares(number_of, total, bound, skew, full):
    weights = [(1 << 20) // math.isqrt(standing ** skew) + 1 for standing in range(1, number_of + 1)]
    largest = bound if full else min(bound, max(-(-total // number_of), total * weights[0] // sum(weights)))
    least = 1 if total - largest >= number_of - 1 else 0
    holding, spare = [largest] + [least] * (number_of - 1), total - largest - least * (number_of - 1)
    while spare > 0:
        free = [i for i in range(1, number_of) if holding[i] < largest] or [i for i in range(1, number_of) if holding[i] < bound]
        mass, budget = sum([weights[i] for i in free]), spare
        for i in free:
            more = min(bound - holding[i], max(1, budget * weights[i] // mass), spare)
            holding[i] = holding[i] + more
            spare = spare - more
    return np.array(holding)


def centred(stream_key, dims, scale, most, split=(), held_as=jnp.bfloat16):
    level = block_scale(stream_key, dims, split, -0.22, 0.18) if split else 1.0
    entries = jax.random.normal(stream_key, dims, jnp.float32) * scale * level
    return jnp.minimum(jnp.maximum(entries, -most), most).astype(held_as)


def setup_inputs(seed: int = 0) -> dict:
    streams_of = jax.random.split(jax.random.key(seed), 11)
    atmos = centred(streams_of[0], (ENSEMBLE_COUNT, LEVELS, NCOL), 1.0, 6.0, ((0, 4), (2, 64)))
    land = centred(streams_of[1], (ENSEMBLE_COUNT, LAYERS, NTILE), 1.0, 6.0, ((0, 4), (2, 64)))
    land_mask = set_ends((jax.random.randint(streams_of[2], (NTILE,), 0, 5) < 3).astype(jnp.int32), jax.random.fold_in(streams_of[2], 1), 0, 1)
    tile_owner_keys = jax.random.split(jax.random.fold_in(streams_of[3], 1), NTILE // TILE_DEV)
    tile_owner_turns = jax.random.permutation(jax.random.fold_in(streams_of[3], 3), NTILE // TILE_DEV)
    tile_owner = jax.vmap(lambda own, number: assign_block(jax.random.fold_in(streams_of[3], 2), own, number, TILE_DEV, N_PATCH, 1, 2 * TILE_DEV // N_PATCH, 2))(tile_owner_keys, tile_owner_turns).reshape((NTILE, 1))
    tile_column = set_ends(jax.random.randint(streams_of[4], (NTILE,), 0, COL_DEV), jax.random.fold_in(streams_of[4], 1), 0, COL_DEV - 1).astype(jnp.int32)
    tile_weight = jnp.clip(0.19921875 + 0.80078125 * jax.random.uniform(streams_of[5], (NTILE,), jnp.float32) ** block_scale(streams_of[5], (NTILE,), ((0, 64),), -0.2, 0.2), 0.19921875, 1.0).astype(jnp.bfloat16)
    obs_value = centred(streams_of[6], (NOBS,), 2.0, 12.0, ((0, 64),), jnp.float32)
    observation_column = set_ends(jax.random.randint(streams_of[7], (NOBS,), 0, COL_DEV), jax.random.fold_in(streams_of[7], 1), 0, COL_DEV - 1).astype(jnp.int32)
    obs_error = jnp.clip(jnp.exp(math.log(4.0) - 2.0794415 * jax.random.uniform(streams_of[8], (NOBS,), jnp.float32) ** block_scale(streams_of[8], (NOBS,), ((0, 64),), -0.2, 0.2)), 0.5, 4.0)
    loc_blocks = draw_loc_blocks(jax.random.fold_in(streams_of[10], 71), 0)
    return dict(atmos=atmos, land=land, land_mask=land_mask, tile_owner=tile_owner, tile_column=tile_column, tile_weight=tile_weight, obs_value=obs_value, observation_column=observation_column, obs_error=obs_error, loc_blocks=loc_blocks)


PRECISE = lax.Precision.HIGHEST

def place_tiles(owners, npatch, bucket):
    onehot = (owners[:, None] == jnp.arange(npatch, dtype=jnp.int32)[None, :]).astype(jnp.int32)
    before = lax.optimization_barrier(jnp.sum((jnp.cumsum(onehot, axis=0) - onehot) * onehot, axis=1))
    return (owners * bucket + before).astype(jnp.int32)

def settle(local_gram, local_proj):
    members = local_gram.shape[0]
    identity = jnp.eye(members, dtype=jnp.float32)
    system = local_gram + (members - 1.0) * identity
    trace_scale = jnp.trace(system)
    upper_iter = system / trace_scale
    lower_iter = identity
    for sweep_index in range(SWEEPS):
        middle_step = 0.5 * (3.0 * identity - jnp.dot(lower_iter, upper_iter, precision=PRECISE))
        upper_iter = jnp.dot(upper_iter, middle_step, precision=PRECISE)
        lower_iter = jnp.dot(middle_step, lower_iter, precision=PRECISE)
    inv_root = lower_iter / jnp.sqrt(trace_scale)
    mean_shift = jnp.dot(inv_root, jnp.dot(inv_root, local_proj, precision=PRECISE), precision=PRECISE)
    spread = mean_shift[:, None] + math.sqrt(members - 1.0) * inv_root
    centered = spread - lax.optimization_barrier(jnp.mean(spread, axis=0, keepdims=True))
    return (centered + 1.0 / members).astype(jnp.bfloat16)

def reference(atmos, land, land_mask, tile_owner, tile_column, tile_weight, obs_value, observation_column, obs_error, loc_blocks):
    owners = tile_owner[:, 0].astype(jnp.int32)
    keep_land = land_mask.astype(jnp.float32)
    weighted = (land[:, 0, :].astype(jnp.float32) * (tile_weight.astype(jnp.float32) * keep_land)[None, :]).astype(jnp.bfloat16)
    target = (owners * COL_DEV + tile_column).astype(jnp.int32)
    land_sum = jax.ops.segment_sum(weighted.astype(jnp.float32).T, target, num_segments=NCOL)
    screen_level = atmos[:, 0, :].astype(jnp.float32) + land_sum.T
    observation_cells = (jnp.arange(NOBS, dtype=jnp.int32) // PATCH_OBS_COUNT * COL_DEV + observation_column).astype(jnp.int32)
    prior_state = lax.optimization_barrier(jnp.take(screen_level, observation_cells, axis=1).astype(jnp.bfloat16))
    block_list = prior_state.astype(jnp.float32).reshape(ENSEMBLE_COUNT, N_PATCH, PATCH_OBS_COUNT)
    center = lax.optimization_barrier(jnp.mean(block_list, axis=0))
    inverse_sd = lax.rsqrt(obs_error.reshape(N_PATCH, PATCH_OBS_COUNT))
    scaled = (block_list - center[None]) * inverse_sd[None]
    innovation = (obs_value.reshape(N_PATCH, PATCH_OBS_COUNT) - center) * inverse_sd
    grams = jnp.einsum('kqo,jqo->qkj', scaled, scaled, precision=PRECISE)
    projs = jnp.einsum('kqo,qo->qk', scaled, innovation, precision=PRECISE)
    counts = lax.optimization_barrier(jnp.sum((loc_blocks[:, :, None] == jnp.arange(N_PATCH, dtype=jnp.int32)[None, None, :]).astype(jnp.float32), axis=1))
    local_grams = jnp.einsum('pq,qkj->pkj', counts, grams, precision=PRECISE)
    local_projs = jnp.einsum('pq,qk->pk', counts, projs, precision=PRECISE)
    mixes = lax.map(lambda block_pair: settle(block_pair[0], block_pair[1]), (local_grams, local_projs))
    wide_mixes = mixes.astype(jnp.float32)
    atmos_blocks = atmos.astype(jnp.float32).reshape(ENSEMBLE_COUNT, LEVELS, N_PATCH, COL_DEV)
    atmos_analysis = jnp.einsum('pkj,klpc->jlpc', wide_mixes, atmos_blocks, precision=PRECISE)
    atmos_analysis = atmos_analysis.astype(jnp.bfloat16).reshape(ENSEMBLE_COUNT, LEVELS, NCOL)
    land_blocks = jnp.moveaxis(land.reshape(ENSEMBLE_COUNT, LAYERS, N_PATCH, TILE_DEV), 2, 0)
    owner_blocks = owners.reshape(N_PATCH, TILE_DEV)

    def one_block(block_pair):
        row_block, owned = block_pair
        slot_of = place_tiles(owned, N_PATCH, CAP)
        buffer = jnp.zeros((ENSEMBLE_COUNT, LAYERS, N_PATCH * CAP), jnp.float32).at[:, :, slot_of].set(row_block.astype(jnp.float32))
        buffer = buffer.reshape(ENSEMBLE_COUNT, LAYERS, N_PATCH, CAP)
        moved_land = jnp.einsum('pkj,klpc->jlpc', wide_mixes, buffer, precision=PRECISE)
        return moved_land.reshape(ENSEMBLE_COUNT, LAYERS, N_PATCH * CAP)[:, :, slot_of].astype(jnp.bfloat16)
    updated = lax.map(one_block, (land_blocks, owner_blocks))
    updated = jnp.moveaxis(updated, 0, 2).reshape(ENSEMBLE_COUNT, LAYERS, NTILE)
    land_analysis = jnp.where(land_mask[None, None, :] == 1, updated, land)
    return (atmos_analysis, land_analysis)
```

```python
import math

import jax
import jax.numpy as jnp
from jax import lax
from jax.experimental import pallas as pl
from jax.experimental.pallas import tpu as pltpu
from jax.sharding import PartitionSpec as P

SWEEPS = 10
PRECISE = lax.Precision.HIGHEST
BF = jnp.bfloat16
F32 = jnp.float32
I32 = jnp.int32

NN = (((1,), (0,)), ((), ()))
NT = (((1,), (1,)), ((), ()))


def dot(a, b, dims=NN):
    return lax.dot_general(a, b, dims, preferred_element_type=F32)


def iota(shape, axis):
    return lax.broadcasted_iota(I32, shape, axis)


VMEM = pl.BlockSpec(memory_space=pltpu.VMEM)
SMEM = pl.BlockSpec(memory_space=pltpu.SMEM)


def params():
    return pltpu.CompilerParams(vmem_limit_bytes=60 * 1024 * 1024)


def shifted(value, axis, steps):
    count = lax.axis_size(axis)
    pairs = [(source, (source + steps) % count) for source in range(count)]
    return lax.ppermute(value, axis, pairs)


def order_tiles(owners, npatch):
    tiles = owners.shape[1]
    block = 512

    def kernel(owner_ref, rank_ref, pos_ref, start_ref):
        before = (iota((block, block), 0) < iota((block, block), 1)).astype(BF)
        carry = jnp.zeros((npatch, 1), F32)
        for c in range(tiles // block):
            cut = slice(c * block, (c + 1) * block)
            hot = owner_ref[:, cut] == iota((npatch, block), 0)
            ahead = dot(hot.astype(BF), before) + carry
            hot32 = hot.astype(F32)
            rank_ref[:, cut] = jnp.sum(hot32 * ahead, axis=0, keepdims=True).astype(I32)
            carry = carry + jnp.sum(hot32, axis=1, keepdims=True)
        lower = (iota((npatch, npatch), 0) > iota((npatch, npatch), 1)).astype(BF)
        wide = dot(lower, jnp.broadcast_to(carry, (npatch, 128)).astype(BF))
        starts = wide[:, :1]
        start_ref[...] = starts.astype(I32)
        for c in range(tiles // block):
            cut = slice(c * block, (c + 1) * block)
            hot = (owner_ref[:, cut] == iota((npatch, block), 0)).astype(F32)
            first = jnp.sum(hot * starts, axis=0, keepdims=True).astype(I32)
            pos_ref[:, cut] = rank_ref[:, cut] + first

    return pl.pallas_call(
        kernel,
        out_shape=(
            jax.ShapeDtypeStruct((1, tiles), I32),
            jax.ShapeDtypeStruct((1, tiles), I32),
            jax.ShapeDtypeStruct((npatch, 1), I32),
        ),
        in_specs=[VMEM],
        out_specs=(VMEM, VMEM, VMEM),
        compiler_params=params(),
        name="order_tiles",
    )(owners)


def bucket_tiles(weighted, owners, ranks, columns, npatch, bucket):
    rows, tiles = weighted.shape
    low = 4
    high = npatch // low
    block = 1024
    steps = tiles // block

    def kernel(w_ref, owner_ref, rank_ref, col_ref, out_ref, acc_ref, cacc_ref):
        step = pl.program_id(0)
        owner = owner_ref[...]
        slot = (owner & (low - 1)) * bucket + rank_ref[...]
        hot = (iota((low * bucket, block), 0) == slot).astype(F32).astype(BF)
        group = owner >> 2
        value = w_ref[...]
        zero = jnp.zeros_like(value)
        picked = jnp.concatenate(
            [jnp.where(group == g, value, zero) for g in range(high)], axis=0
        )
        part = dot(picked, hot, NT)
        col = col_ref[...]
        half = iota((2 * high, block), 0)
        digit = jnp.where((half & 1) == 0, col >> 5, col & 31)
        digits = jnp.where((half >> 1) == group, digit, 0).astype(F32).astype(BF)
        cpart = dot(digits, hot, NT)

        @pl.when(step == 0)
        def _():
            acc_ref[...] = part
            cacc_ref[...] = cpart

        @pl.when(step > 0)
        def _():
            acc_ref[...] += part
            cacc_ref[...] += cpart

        @pl.when(step == steps - 1)
        def _():
            for o in range(npatch):
                g, b = o // low, o % low
                cut = slice(b * bucket, (b + 1) * bucket)
                out_ref[o, :rows, :] = acc_ref[g * rows : (g + 1) * rows, cut].astype(BF)
                out_ref[o, rows : rows + 2, :] = cacc_ref[2 * g : 2 * g + 2, cut].astype(BF)

    lane = pl.BlockSpec((1, block), lambda i: (0, i))
    return pl.pallas_call(
        kernel,
        grid=(steps,),
        out_shape=jax.ShapeDtypeStruct((npatch, rows + 2, bucket), BF),
        in_specs=[pl.BlockSpec((rows, block), lambda i: (0, i)), lane, lane, lane],
        out_specs=pl.BlockSpec((npatch, rows + 2, bucket), lambda i: (0, 0, 0)),
        scratch_shapes=[
            pltpu.VMEM((high * rows, low * bucket), F32),
            pltpu.VMEM((2 * high, low * bucket), F32),
        ],
        compiler_params=params(),
        name="bucket_tiles",
    )(weighted, owners, ranks, columns)


def lane_swap(rows, a, b):
    source = iota((rows, rows), 0)
    target = iota((rows, rows), 1)
    return ((source % b) * a + source // b == target).astype(F32).astype(BF)


def sort_land(pos, land_rows, levels):
    rows, tiles = land_rows.shape
    block = 512

    def kernel(pos_ref, x_ref, out_ref):
        place = iota((block, tiles), 0) + pl.program_id(0) * block
        hot = (place == pos_ref[...]).astype(F32).astype(BF)
        moved = dot(hot, x_ref[...], NT).astype(BF)
        out_ref[...] = dot(moved, lane_swap(rows, rows // levels, levels)).astype(BF)

    return pl.pallas_call(
        kernel,
        grid=(tiles // block,),
        out_shape=jax.ShapeDtypeStruct((tiles, rows), BF),
        in_specs=[
            pl.BlockSpec((1, tiles), lambda i: (0, 0)),
            pl.BlockSpec((rows, tiles), lambda i: (0, 0)),
        ],
        out_specs=pl.BlockSpec((block, rows), lambda i: (i, 0)),
        compiler_params=params(),
        name="sort_land",
    )(pos, land_rows)


def screen_forecast(received, base, obs_column):
    npatch, rows2, bucket = received.shape
    rows = rows2 - 2
    nobs = obs_column.shape[0]
    columns = base.shape[1]
    group = 8

    def kernel(in_ref, base_ref, obs_ref, out_ref):
        obs = obs_ref[...]
        place = iota((nobs, columns), 1)
        acc = dot(base_ref[...], (obs == place).astype(F32).astype(BF), NT)
        for g in range(npatch // group):
            values = jnp.concatenate(
                [in_ref[g * group + i, :rows, :] for i in range(group)], axis=1
            )
            digits = jnp.concatenate(
                [in_ref[g * group + i, rows:, :] for i in range(group)], axis=1
            ).astype(F32)
            col = (digits[0:1] * 32.0 + digits[1:2]).astype(I32)
            acc = acc + dot(values, (obs == col).astype(F32).astype(BF), NT)
        out_ref[...] = acc.astype(BF)

    return pl.pallas_call(
        kernel,
        out_shape=jax.ShapeDtypeStruct((rows, nobs), BF),
        in_specs=[VMEM, VMEM, VMEM],
        out_specs=VMEM,
        compiler_params=params(),
        name="screen_forecast",
    )(received, base, obs_column)


def mix_land(states, sources, starts, mixes, pos_col, land_rows, mask_row, levels):
    slots = len(states)
    tiles, width = states[0].shape
    local = width // levels
    npatch = mixes.shape[0]
    members = mixes.shape[2]
    window = 144
    block = 512

    def kernel(src_ref, start_ref, *refs):
        state_refs = refs[:slots]
        mix_ref, pos_ref, land_ref, mask_ref, out_ref, tiled_ref, y_ref, z_ref = refs[slots:]

        @pl.when(pl.program_id(0) == 0)
        def _():
            for s in range(slots):
                spread = (
                    iota((members, width), 0)
                    == (iota((members, width), 1) & (local - 1)) + src_ref[s] * local
                )
                tiled_ref[:, s * width : (s + 1) * width] = dot(
                    mix_ref[...], spread.astype(F32).astype(BF)
                ).astype(BF)
            y_ref[...] = jnp.zeros_like(y_ref)
            lane_level = iota((local, width), 1) // local

            def one_owner(o, unused):
                first = start_ref[o]
                base = pl.multiple_of(
                    jnp.minimum((first // 16) * 16, tiles - window), 16
                )
                acc = jnp.zeros((window, width), F32)
                for s in range(slots):
                    small = tiled_ref[
                        pl.ds(pl.multiple_of(o * local, local), local),
                        s * width : (s + 1) * width,
                    ]
                    zero = jnp.zeros_like(small)
                    weight = jnp.concatenate(
                        [jnp.where(lane_level == l, small, zero) for l in range(levels)], axis=0
                    )
                    acc = acc + dot(state_refs[s][pl.ds(base, window), :], weight, NT)
                value = acc.astype(BF)
                rest = y_ref[pl.ds(base, window), :]
                y_ref[pl.ds(base, window), :] = jnp.where(
                    iota((window, width), 0) + base >= first, value, rest
                )
                return unused

            lax.fori_loop(0, npatch, one_owner, 0)
            z_ref[...] = dot(y_ref[...], lane_swap(width, levels, local)).astype(BF)

        hot = (iota((block, tiles), 1) == pos_ref[...]).astype(F32).astype(BF)
        back = dot(hot, z_ref[...])
        out_ref[...] = jnp.where(mask_ref[...] == 1, back.T.astype(BF), land_ref[...])

    full = lambda shape: pl.BlockSpec(shape, lambda i: (0,) * len(shape))
    return pl.pallas_call(
        kernel,
        grid=(tiles // block,),
        out_shape=jax.ShapeDtypeStruct((width, tiles), BF),
        in_specs=[SMEM, SMEM]
        + [VMEM] * slots
        + [
            VMEM,
            pl.BlockSpec((block, 1), lambda i: (i, 0)),
            pl.BlockSpec((width, block), lambda i: (0, i)),
            pl.BlockSpec((1, block), lambda i: (0, i)),
        ],
        out_specs=pl.BlockSpec((width, block), lambda i: (0, i)),
        scratch_shapes=[
            pltpu.VMEM((npatch * local, slots * width), BF),
            pltpu.VMEM((tiles, width), BF),
            pltpu.VMEM((tiles, width), BF),
        ],
        compiler_params=params(),
        name="mix_land",
    )(
        sources,
        starts,
        *states,
        mixes.reshape(npatch * local, members),
        pos_col,
        land_rows,
        mask_row,
    )


def settle(local_gram, local_proj):
    members = local_gram.shape[0]
    identity = jnp.eye(members, dtype=jnp.float32)
    system = local_gram + (members - 1.0) * identity
    trace_scale = jnp.trace(system)
    upper_iter = system / trace_scale
    lower_iter = identity
    for sweep_index in range(SWEEPS):
        middle_step = 0.5 * (3.0 * identity - jnp.dot(lower_iter, upper_iter, precision=PRECISE))
        upper_iter = jnp.dot(upper_iter, middle_step, precision=PRECISE)
        lower_iter = jnp.dot(middle_step, lower_iter, precision=PRECISE)
    inv_root = lower_iter / jnp.sqrt(trace_scale)
    mean_shift = jnp.dot(
        inv_root, jnp.dot(inv_root, local_proj, precision=PRECISE), precision=PRECISE
    )
    spread = mean_shift[:, None] + math.sqrt(members - 1.0) * inv_root
    centered = spread - jnp.mean(spread, axis=0, keepdims=True)
    return (centered + 1.0 / members).astype(jnp.bfloat16)


def to_all(value, axis):
    count = lax.axis_size(axis)
    copies = jnp.broadcast_to(value[None], (count,) + value.shape)
    return lax.all_to_all(copies, axis, split_axis=0, concat_axis=0, tiled=True)


def shards(
    atmos,
    land,
    land_mask,
    tile_owner,
    tile_column,
    tile_weight,
    obs_value,
    observation_column,
    obs_error,
    loc_blocks,
):
    npatch = lax.axis_size("patch")
    mem_count = lax.axis_size("mem")
    local, levels, columns = atmos.shape
    layers, tiles = (land.shape[1], land.shape[2])
    members = local * mem_count
    bucket = 2 * tiles // npatch
    row_width = max(2, npatch // 8)
    mem_rank = lax.axis_index("mem")
    patch_rank = lax.axis_index("patch")

    atmos_rows = atmos.reshape(local * levels, columns)
    atmos_parts = [atmos_rows] + [shifted(atmos_rows, "mem", s) for s in (1, -1, 2)]

    owners = tile_owner.reshape(1, tiles)
    ranks, pos, starts = order_tiles(owners, npatch)
    keep = tile_weight.astype(F32) * land_mask.astype(F32)
    weighted = (land[:, 0, :].astype(F32) * keep[None, :]).astype(BF)
    packed = bucket_tiles(
        weighted, owners, ranks, tile_column.reshape(1, tiles), npatch, bucket
    )
    received = lax.all_to_all(packed, "patch", split_axis=0, concat_axis=0, tiled=True)

    land_rows = land.reshape(local * layers, tiles)
    mine = sort_land(pos, land_rows, layers)
    half = tiles // 2
    from_prev = shifted(mine, "mem", 1)
    from_next = shifted(mine, "mem", -1)

    forecast = screen_forecast(received, atmos[:, 0, :], observation_column.reshape(-1, 1))
    ensemble = to_all(forecast, "mem").reshape(members, -1).astype(F32)
    center = jnp.mean(ensemble, axis=0)
    inverse_sd = lax.rsqrt(obs_error)
    scaled = (ensemble - center[None, :]) * inverse_sd[None, :]
    innovation = (obs_value - center) * inverse_sd
    gram_own = jnp.dot(scaled, scaled.T, precision=PRECISE)
    proj_own = jnp.dot(scaled, innovation, precision=PRECISE)
    listed = loc_blocks[0]
    own_stats = jnp.concatenate([gram_own, proj_own[None, :]], axis=0)
    local_stats = own_stats
    for offset in (1, -1, row_width, -row_width):
        near_stats = shifted(own_stats, "patch", offset)
        source = (patch_rank - offset) % npatch
        used = jnp.sum((listed == source).astype(jnp.float32))
        local_stats = local_stats + used * near_stats
    local_stats, from_prev, from_next = lax.optimization_barrier(
        (local_stats, from_prev, from_next)
    )
    far_low = shifted(from_prev[:half], "mem", 1)
    far_high = shifted(from_next[half:], "mem", -1)
    mix = settle(local_stats[:members], local_stats[members])
    mix_t = mix.T

    own_cols = lax.dynamic_slice_in_dim(mix_t, mem_rank * local, local, 0)
    all_mixes = to_all(own_cols, "patch")

    slot_source = [mem_rank, mem_rank - 1, mem_rank + 1, mem_rank - 2]
    sources = jnp.stack([s % mem_count for s in slot_source]).astype(I32)
    atmos_out = 0.0
    for part, source in zip(atmos_parts, slot_source):
        rows = lax.dynamic_slice_in_dim(own_cols, (source % mem_count) * local, local, 1)
        atmos_out = atmos_out + jnp.einsum(
            "jk,klc->jlc", rows, part.reshape(local, levels, columns), preferred_element_type=F32
        )
    atmos_analysis = atmos_out.astype(BF)

    far = jnp.concatenate([far_low, far_high], axis=0)
    land_out = mix_land(
        [mine, from_prev, from_next, far],
        sources,
        starts.reshape(npatch),
        all_mixes,
        pos.reshape(tiles, 1),
        land_rows,
        land_mask.reshape(1, tiles),
        layers,
    )
    return (atmos_analysis, land_out.reshape(local, layers, tiles))


def solution(mesh):
    in_specs = (
        P("mem", None, "patch"),
        P("mem", None, "patch"),
        P("patch"),
        P("patch", None),
        P("patch"),
        P("patch"),
        P("patch"),
        P("patch"),
        P("patch"),
        P("patch", None),
    )
    out_specs = (P("mem", None, "patch"), P("mem", None, "patch"))
    return jax.shard_map(shards, mesh=mesh, in_specs=in_specs, out_specs=out_specs, check_vma=False)
```

```python
import math

import jax
import jax.numpy as jnp
from jax import lax
from jax.experimental import pallas as pl
from jax.experimental.pallas import tpu as pltpu
from jax.sharding import PartitionSpec as P

SWEEPS = 10
PRECISE = lax.Precision.HIGHEST
BF = jnp.bfloat16
F32 = jnp.float32
I32 = jnp.int32

NN = (((1,), (0,)), ((), ()))
NT = (((1,), (1,)), ((), ()))


def dot(a, b, dims=NN):
    return lax.dot_general(a, b, dims, preferred_element_type=F32)


def iota(shape, axis):
    return lax.broadcasted_iota(I32, shape, axis)


VMEM = pl.BlockSpec(memory_space=pltpu.VMEM)
SMEM = pl.BlockSpec(memory_space=pltpu.SMEM)


def params(mib):
    return pltpu.CompilerParams(vmem_limit_bytes=mib * 1024 * 1024)


def shifted(value, axis, steps):
    count = lax.axis_size(axis)
    pairs = [(source, (source + steps) % count) for source in range(count)]
    return lax.ppermute(value, axis, pairs)


PARTS = 4
UNROLL = 4


def order_tiles(owners, npatch):
    tiles = owners.shape[1]
    block = 512
    per_part = tiles // PARTS // block

    def kernel(owner_ref, rank_ref, pos_ref, start_ref):
        before = (iota((block, block), 0) < iota((block, block), 1)).astype(BF)
        lower = (iota((npatch, npatch), 0) > iota((npatch, npatch), 1)).astype(BF)
        done = jnp.zeros((npatch, 1), F32)
        for part in range(PARTS):
            carry = jnp.zeros((npatch, 1), F32)
            held = []
            for c in range(per_part):
                at = (part * per_part + c) * block
                hot = owner_ref[:, at : at + block] == iota((npatch, block), 0)
                ahead = dot(hot.astype(BF), before) + carry
                hot = hot.astype(F32)
                carry = carry + jnp.sum(hot, axis=1, keepdims=True)
                held.append((at, hot, ahead))
            starts = dot(lower, jnp.broadcast_to(carry, (npatch, 128)).astype(BF))[:, :1]
            start_ref[:, part : part + 1] = starts.astype(I32)
            for at, hot, ahead in held:
                rank = jnp.sum(hot * (ahead + done), axis=0, keepdims=True)
                pos = jnp.sum(hot * (ahead + starts), axis=0, keepdims=True)
                rank_ref[:, at : at + block] = rank.astype(I32)
                pos_ref[:, at : at + block] = pos.astype(I32)
            done = done + carry
        start_ref[:, PARTS:] = jnp.zeros((npatch, PARTS), I32)

    return pl.pallas_call(
        kernel,
        out_shape=(
            jax.ShapeDtypeStruct((1, tiles), I32),
            jax.ShapeDtypeStruct((1, tiles), I32),
            jax.ShapeDtypeStruct((npatch, 2 * PARTS), I32),
        ),
        in_specs=[VMEM],
        out_specs=(VMEM, VMEM, VMEM),
        compiler_params=params(60),
        name="order_tiles",
    )(owners)


def bucket_tiles(land_rows, levels, weight, mask, owners, ranks, columns, npatch, bucket):
    width, tiles = land_rows.shape
    rows = width // levels
    low = 4
    high = npatch // low
    block = 1024
    steps = tiles // block

    def kernel(
        x_ref, weight_ref, mask_ref, owner_ref, rank_ref, col_ref, out_ref, acc_ref, cacc_ref
    ):
        step = pl.program_id(0)
        owner = owner_ref[...]
        slot = (owner & (low - 1)) * bucket + rank_ref[...]
        hot = (iota((low * bucket, block), 0) == slot).astype(F32).astype(BF)
        group = owner >> 2
        surface = (iota((rows, width), 0) * levels == iota((rows, width), 1)).astype(F32)
        keep = weight_ref[...].astype(F32) * mask_ref[...].astype(F32)
        value = (dot(surface.astype(BF), x_ref[...]) * keep).astype(BF)
        zero = jnp.zeros_like(value)
        picked = jnp.concatenate(
            [jnp.where(group == g, value, zero) for g in range(high)], axis=0
        )
        part = dot(picked, hot, NT)
        col = col_ref[...]
        half = iota((2 * high, block), 0)
        digit = jnp.where((half & 1) == 0, col >> 5, col & 31)
        digits = jnp.where((half >> 1) == group, digit, 0).astype(F32).astype(BF)
        cpart = dot(digits, hot, NT)

        @pl.when(step == 0)
        def _():
            acc_ref[...] = part
            cacc_ref[...] = cpart

        @pl.when(step > 0)
        def _():
            acc_ref[...] += part
            cacc_ref[...] += cpart

        @pl.when(step == steps - 1)
        def _():
            for o in range(npatch):
                g, b = o // low, o % low
                cut = slice(b * bucket, (b + 1) * bucket)
                out_ref[o, :rows, :] = acc_ref[g * rows : (g + 1) * rows, cut].astype(BF)
                out_ref[o, rows : rows + 2, :] = cacc_ref[2 * g : 2 * g + 2, cut].astype(BF)

    lane = pl.BlockSpec((1, block), lambda i: (0, i))
    return pl.pallas_call(
        kernel,
        grid=(steps,),
        out_shape=jax.ShapeDtypeStruct((npatch, rows + 2, bucket), BF),
        in_specs=[pl.BlockSpec((width, block), lambda i: (0, i))] + [lane] * 5,
        out_specs=pl.BlockSpec((npatch, rows + 2, bucket), lambda i: (0, 0, 0)),
        scratch_shapes=[
            pltpu.VMEM((high * rows, low * bucket), F32),
            pltpu.VMEM((2 * high, low * bucket), F32),
        ],
        compiler_params=params(60),
        name="bucket_tiles",
    )(land_rows, weight, mask, owners, ranks, columns)


def lane_swap(rows, a, b):
    source = iota((rows, rows), 0)
    target = iota((rows, rows), 1)
    return ((source % b) * a + source // b == target).astype(F32).astype(BF)


def sort_land(pos, land_rows, levels, first):
    width, tiles = land_rows.shape
    span = tiles // PARTS
    block = 512

    def kernel(pos_ref, x_ref, low_ref, high_ref):
        swap = lane_swap(width, width // levels, levels)
        for c in range(tiles // block):
            part = c * block // span
            cut = slice(part * span, (part + 1) * span)
            place = iota((block, span), 0) + (c * block - part * span)
            hot = (place == pos_ref[:, cut]).astype(F32).astype(BF)
            moved = dot(hot, x_ref[:, cut], NT).astype(BF)
            value = dot(moved, swap).astype(BF)
            at = c * block
            if at < first:
                low_ref[at : at + block, :] = value
            else:
                high_ref[at - first : at - first + block, :] = value

    return pl.pallas_call(
        kernel,
        out_shape=(
            jax.ShapeDtypeStruct((first, width), BF),
            jax.ShapeDtypeStruct((tiles - first, width), BF),
        ),
        in_specs=[VMEM, VMEM],
        out_specs=(VMEM, VMEM),
        compiler_params=params(60),
        name="sort_land",
    )(pos, land_rows)


def screen_forecast(received, base_rows, levels, obs_column):
    npatch, rows2, _ = received.shape
    rows = rows2 - 2
    nobs = obs_column.shape[0]
    width, columns = base_rows.shape
    group = 8

    def kernel(in_ref, base_ref, obs_ref, out_ref):
        obs = obs_ref[...]
        place = iota((nobs, columns), 1)
        surface = (iota((rows, width), 0) * levels == iota((rows, width), 1)).astype(F32)
        base = dot(surface.astype(BF), base_ref[...]).astype(BF)
        acc = dot(base, (obs == place).astype(F32).astype(BF), NT)
        for g in range(npatch // group):
            values = jnp.concatenate(
                [in_ref[g * group + i, :rows, :] for i in range(group)], axis=1
            )
            digits = jnp.concatenate(
                [in_ref[g * group + i, rows:, :] for i in range(group)], axis=1
            ).astype(F32)
            col = (digits[0:1] * 32.0 + digits[1:2]).astype(I32)
            acc = acc + dot(values, (obs == col).astype(F32).astype(BF), NT)
        out_ref[...] = acc.astype(BF)

    return pl.pallas_call(
        kernel,
        out_shape=jax.ShapeDtypeStruct((rows, nobs), BF),
        in_specs=[VMEM, VMEM, VMEM],
        out_specs=VMEM,
        compiler_params=params(60),
        name="screen_forecast",
    )(received, base_rows, obs_column)


def mix_land(pieces, sources, starts, mixes, pos_col, land_rows, mask_row, levels):
    slots = len(pieces)
    flat = [piece for group in pieces for piece in group]
    places = [
        (s, sum(p.shape[0] for p in group[:i]))
        for s, group in enumerate(pieces)
        for i in range(len(group))
    ]
    width, tiles = land_rows.shape
    local = width // levels
    npatch = mixes.shape[0]
    members = mixes.shape[2]
    span = tiles // PARTS
    window = 48
    lanes = 128
    count = len(flat)

    def kernel(src_ref, start_ref, *refs):
        piece_refs = refs[:count]
        mix_ref, pos_ref, land_ref, mask_ref, out_ref = refs[count : count + 5]
        state_ref, tiled_ref, y_ref, sems = refs[count + 5 :]
        step = pl.program_id(0)

        @pl.when(step == 0)
        def _():
            copies = [
                pltpu.make_async_copy(
                    piece_refs[i],
                    state_ref.at[s, pl.ds(at, piece_refs[i].shape[0]), :],
                    sems.at[i],
                )
                for i, (s, at) in enumerate(places)
            ]
            for copy in copies:
                copy.start()
            for s in range(slots):
                spread = (
                    iota((members, lanes), 0)
                    == (iota((members, lanes), 1) & (local - 1)) + src_ref[s] * local
                )
                tiled_ref[:, s * lanes : (s + 1) * lanes] = dot(
                    mix_ref[...], spread.astype(F32).astype(BF)
                ).astype(BF)
            lane_level = iota((local, lanes), 1) // local
            y_ref[...] = jnp.zeros_like(y_ref)
            for copy in copies:
                copy.wait()

            def weight_of(o, s):
                at = pl.multiple_of(o * local, local)
                parts = []
                for t in (s, s + 1):
                    small = tiled_ref[pl.ds(at, local), t * lanes : (t + 1) * lanes]
                    zero = jnp.zeros_like(small)
                    parts += [
                        jnp.where(lane_level == l, small, zero) for l in range(lanes // local)
                    ]
                return jnp.concatenate(parts, axis=0)

            def mixed(o, cuts):
                acc = None
                for s in range(0, slots, 2):
                    rows = [
                        jnp.concatenate(
                            [
                                state_ref[t, pl.ds(at, window), h * lanes : (h + 1) * lanes]
                                for t in (s, s + 1)
                            ],
                            axis=1,
                        )
                        for h in range(width // lanes)
                        for at in cuts
                    ]
                    part = dot(jnp.concatenate(rows, axis=0), weight_of(o, s))
                    acc = part if acc is None else acc + part
                half = len(cuts) * window
                return jnp.concatenate(
                    [acc[h * half : (h + 1) * half] for h in range(width // lanes)], axis=1
                ).astype(BF)

            def put(part, base, first, end, value):
                at = pl.multiple_of(part * span + base, 16)
                row = iota((window, width), 0) + base
                keep = row >= first
                if end is not None:
                    keep = jnp.logical_and(keep, row < end)
                old = y_ref[pl.ds(at, window), :]
                y_ref[pl.ds(at, window), :] = jnp.where(keep, value, old)

            def begin(first):
                return pl.multiple_of(jnp.minimum((first // 16) * 16, span - window), 16)

            def bounds(o):
                firsts = [start_ref[o, q] for q in range(PARTS)]
                after = jnp.minimum(o + 1, npatch - 1)
                ends = [
                    jnp.where(o == npatch - 1, span, start_ref[after, q]) for q in range(PARTS)
                ]
                return firsts, ends, [begin(first) for first in firsts]

            def owners(i, unused):
                group = [i * UNROLL + u for u in range(UNROLL)]
                limits = [bounds(o) for o in group]
                values = [
                    mixed(o, [pl.multiple_of(q * span + bases[q], 16) for q in range(PARTS)])
                    for o, (firsts, ends, bases) in zip(group, limits)
                ]
                for value, (firsts, ends, bases) in zip(values, limits):
                    for q in range(PARTS):
                        put(q, bases[q], firsts[q], None, value[q * window : (q + 1) * window])
                most = 0
                for firsts, ends, bases in limits:
                    for q in range(PARTS):
                        most = jnp.maximum(most, ends[q] - bases[q] - window)

                @pl.when(most > 0)
                def _():
                    for o, (firsts, ends, bases) in zip(group, limits):
                        for q in range(PARTS):

                            def more(n, unused, o=o, q=q, first=firsts[q], end=ends[q], low=bases[q]):
                                base = begin(low + (n + 1) * window)
                                at = pl.multiple_of(q * span + base, 16)
                                put(q, base, first, end, mixed(o, [at]))
                                return unused

                            lack = jnp.maximum(ends[q] - bases[q] - window, 0)
                            lax.fori_loop(0, (lack + window - 1) // window, more, 0)

                return unused

            lax.fori_loop(0, npatch // UNROLL, owners, 0)

        hot = (iota((span, span), 1) == pos_ref[...]).astype(F32).astype(BF)
        rows = y_ref[pl.ds(pl.multiple_of(step * span, span), span), :]
        rows = dot(rows, lane_swap(width, levels, local)).astype(BF)
        back = dot(hot, rows)
        out_ref[...] = jnp.where(mask_ref[...] == 1, back.T.astype(BF), land_ref[...])

    return pl.pallas_call(
        kernel,
        grid=(PARTS,),
        out_shape=jax.ShapeDtypeStruct((width, tiles), BF),
        in_specs=[SMEM, SMEM]
        + [pl.BlockSpec(memory_space=pl.ANY)] * count
        + [
            VMEM,
            pl.BlockSpec((span, 1), lambda i: (i, 0)),
            pl.BlockSpec((width, span), lambda i: (0, i)),
            pl.BlockSpec((1, span), lambda i: (0, i)),
        ],
        out_specs=pl.BlockSpec((width, span), lambda i: (0, i)),
        scratch_shapes=[
            pltpu.VMEM((slots, tiles, width), BF),
            pltpu.VMEM((npatch * local, slots * lanes), BF),
            pltpu.VMEM((tiles, width), BF),
            pltpu.SemaphoreType.DMA((count,)),
        ],
        compiler_params=params(60),
        name="mix_land",
    )(
        sources,
        starts,
        *flat,
        mixes.reshape(npatch * local, members),
        pos_col,
        land_rows,
        mask_row,
    )


def settle(local_gram, local_proj):
    members = local_gram.shape[0]
    identity = jnp.eye(members, dtype=jnp.float32)
    system = local_gram + (members - 1.0) * identity
    trace_scale = jnp.trace(system)
    upper_iter = system / trace_scale
    lower_iter = identity
    for _ in range(SWEEPS):
        middle_step = 0.5 * (3.0 * identity - jnp.dot(lower_iter, upper_iter, precision=PRECISE))
        upper_iter = jnp.dot(upper_iter, middle_step, precision=PRECISE)
        lower_iter = jnp.dot(middle_step, lower_iter, precision=PRECISE)
    inv_root = lower_iter / jnp.sqrt(trace_scale)
    mean_shift = jnp.dot(
        inv_root, jnp.dot(inv_root, local_proj, precision=PRECISE), precision=PRECISE
    )
    spread = mean_shift[:, None] + math.sqrt(members - 1.0) * inv_root
    centered = spread - jnp.mean(spread, axis=0, keepdims=True)
    return (centered + 1.0 / members).astype(jnp.bfloat16)


def to_all(value, axis):
    count = lax.axis_size(axis)
    copies = jnp.broadcast_to(value[None], (count,) + value.shape)
    return lax.all_to_all(copies, axis, split_axis=0, concat_axis=0, tiled=True)


def analysis(
    atmos,
    land,
    land_mask,
    tile_owner,
    tile_column,
    tile_weight,
    obs_value,
    observation_column,
    obs_error,
    loc_blocks,
):
    barrier = lax.optimization_barrier
    npatch = lax.axis_size("patch")
    mem_count = lax.axis_size("mem")
    local, levels, columns = atmos.shape
    layers, tiles = (land.shape[1], land.shape[2])
    members = local * mem_count
    bucket = 2 * tiles // npatch
    row_width = max(2, npatch // 8)
    first = 3 * tiles // 8
    mem_rank = lax.axis_index("mem")
    patch_rank = lax.axis_index("patch")

    atmos_rows = atmos.reshape(local * levels, columns)
    atmos_parts = [shifted(atmos_rows, "mem", s) for s in (1, -1, 2)]

    owners = tile_owner.reshape(1, tiles)
    land_rows = land.reshape(local * layers, tiles)
    mask_row = land_mask.reshape(1, tiles)
    ranks, pos, starts = order_tiles(owners, npatch)
    packed = bucket_tiles(
        land_rows,
        layers,
        tile_weight.reshape(1, tiles),
        mask_row,
        owners,
        ranks,
        tile_column.reshape(1, tiles),
        npatch,
        bucket,
    )
    received = lax.all_to_all(packed, "patch", split_axis=0, concat_axis=0, tiled=True)

    low, high = sort_land(pos, land_rows, layers, first)
    low_prev = shifted(low, "mem", 1)
    low_next = shifted(low, "mem", -1)

    forecast = screen_forecast(received, atmos_rows, levels, observation_column.reshape(-1, 1))
    forecast, low_prev, low_next = barrier((forecast, low_prev, low_next))
    ensemble = to_all(forecast, "mem")
    ensemble, high, low_prev, low_next = barrier((ensemble, high, low_prev, low_next))
    high_prev = shifted(high, "mem", 1)
    high_next = shifted(high, "mem", -1)
    low_far = [
        shifted(low_prev[: first // 2], "mem", 1), shifted(low_next[first // 2 :], "mem", -1)
    ]

    ensemble = ensemble.reshape(members, -1).astype(F32)
    center = jnp.mean(ensemble, axis=0)
    inverse_sd = lax.rsqrt(obs_error)
    scaled = (ensemble - center[None, :]) * inverse_sd[None, :]
    innovation = (obs_value - center) * inverse_sd
    gram_own = jnp.dot(scaled, scaled.T, precision=PRECISE)
    proj_own = jnp.dot(scaled, innovation, precision=PRECISE)
    own_stats = jnp.concatenate([gram_own, proj_own[None, :]], axis=0)
    listed = loc_blocks[0]
    local_stats = own_stats
    for offset in (1, -1, row_width, -row_width):
        near_stats = shifted(own_stats, "patch", offset)
        source = (patch_rank - offset) % npatch
        used = jnp.sum((listed == source).astype(jnp.float32))
        local_stats = local_stats + used * near_stats
    mix = settle(local_stats[:members], local_stats[members])

    own_cols = lax.dynamic_slice_in_dim(mix.T, mem_rank * local, local, 0)
    blocks = own_cols.reshape(local, mem_count, local).transpose(2, 1, 0).reshape(local, members)
    all_mixes = to_all(blocks, "patch")
    own_cols, high_prev, high_next = barrier((own_cols, high_prev, high_next))
    split = high.shape[0] // 2
    high_far = [shifted(high_prev[:split], "mem", 1), shifted(high_next[split:], "mem", -1)]

    slot_source = [mem_rank, mem_rank - 1, mem_rank + 1, mem_rank - 2]
    sources = jnp.stack([s % mem_count for s in slot_source]).astype(I32)
    atmos_out = 0.0
    for part, source in zip([atmos_rows] + atmos_parts, slot_source):
        rows = lax.dynamic_slice_in_dim(own_cols, (source % mem_count) * local, local, 1)
        atmos_out = atmos_out + jnp.einsum(
            "jk,klc->jlc", rows, part.reshape(local, levels, columns), preferred_element_type=F32
        )
    atmos_analysis = atmos_out.astype(BF)

    land_out = mix_land(
        [[low, high], [low_prev, high_prev], [low_next, high_next], low_far + high_far],
        sources,
        starts,
        all_mixes,
        pos.reshape(tiles, 1),
        land_rows,
        mask_row,
        layers,
    )
    return (atmos_analysis, land_out.reshape(local, layers, tiles))


def solution(mesh):
    in_specs = (
        P("mem", None, "patch"),
        P("mem", None, "patch"),
        P("patch"),
        P("patch", None),
        P("patch"),
        P("patch"),
        P("patch"),
        P("patch"),
        P("patch"),
        P("patch", None),
    )
    out_specs = (P("mem", None, "patch"), P("mem", None, "patch"))
    return jax.shard_map(
        analysis, mesh=mesh, in_specs=in_specs, out_specs=out_specs, check_vma=False
    )
```

```python
import math

import jax
import jax.numpy as jnp
from jax import lax
from jax.experimental import pallas as pl
from jax.experimental.pallas import tpu as pltpu
from jax.sharding import PartitionSpec as P

SWEEPS = 10
PRECISE = lax.Precision.HIGHEST
BF = jnp.bfloat16
F32 = jnp.float32
I32 = jnp.int32

NN = (((1,), (0,)), ((), ()))
NT = (((1,), (1,)), ((), ()))


def dot(a, b, dims=NN):
    return lax.dot_general(a, b, dims, preferred_element_type=F32)


def iota(shape, axis):
    return lax.broadcasted_iota(I32, shape, axis)


VMEM = pl.BlockSpec(memory_space=pltpu.VMEM)
SMEM = pl.BlockSpec(memory_space=pltpu.SMEM)


def params(mib):
    return pltpu.CompilerParams(vmem_limit_bytes=mib * 1024 * 1024)


def shifted(value, axis, steps):
    count = lax.axis_size(axis)
    pairs = [(source, (source + steps) % count) for source in range(count)]
    return lax.ppermute(value, axis, pairs)


PARTS = 4
UNROLL = 4


def order_tiles(owners, npatch):
    tiles = owners.shape[1]
    block = 512
    per_part = tiles // PARTS // block

    def kernel(owner_ref, rank_ref, pos_ref, start_ref):
        before = (iota((block, block), 0) < iota((block, block), 1)).astype(BF)
        lower = (iota((npatch, npatch), 0) > iota((npatch, npatch), 1)).astype(BF)
        done = jnp.zeros((npatch, 1), F32)
        for part in range(PARTS):
            carry = jnp.zeros((npatch, 1), F32)
            held = []
            for c in range(per_part):
                at = (part * per_part + c) * block
                hot = owner_ref[:, at : at + block] == iota((npatch, block), 0)
                ahead = dot(hot.astype(BF), before) + carry
                hot = hot.astype(F32)
                carry = carry + jnp.sum(hot, axis=1, keepdims=True)
                held.append((at, hot, ahead))
            starts = dot(lower, jnp.broadcast_to(carry, (npatch, 128)).astype(BF))[:, :1]
            start_ref[:, part : part + 1] = starts.astype(I32)
            for at, hot, ahead in held:
                rank = jnp.sum(hot * (ahead + done), axis=0, keepdims=True)
                pos = jnp.sum(hot * (ahead + starts), axis=0, keepdims=True)
                rank_ref[:, at : at + block] = rank.astype(I32)
                pos_ref[:, at : at + block] = pos.astype(I32)
            done = done + carry
        start_ref[:, PARTS:] = jnp.zeros((npatch, PARTS), I32)

    return pl.pallas_call(
        kernel,
        out_shape=(
            jax.ShapeDtypeStruct((1, tiles), I32),
            jax.ShapeDtypeStruct((1, tiles), I32),
            jax.ShapeDtypeStruct((npatch, 2 * PARTS), I32),
        ),
        in_specs=[VMEM],
        out_specs=(VMEM, VMEM, VMEM),
        compiler_params=params(60),
        name="order_tiles",
    )(owners)


def bucket_tiles(land_rows, levels, weight, owners, ranks, columns, npatch, bucket):
    width, tiles = land_rows.shape
    rows = width // levels
    low = 4
    high = npatch // low
    block = 1024
    steps = tiles // block

    def kernel(
        x_ref, weight_ref, owner_ref, rank_ref, col_ref, out_ref, acc_ref, cacc_ref
    ):
        step = pl.program_id(0)
        owner = owner_ref[...]
        slot = (owner & (low - 1)) * bucket + rank_ref[...]
        hot = (iota((low * bucket, block), 0) == slot).astype(F32).astype(BF)
        group = owner >> 2
        surface = (iota((rows, width), 0) * levels == iota((rows, width), 1)).astype(F32)
        value = (dot(surface.astype(BF), x_ref[...]) * weight_ref[...]).astype(BF)
        zero = jnp.zeros_like(value)
        picked = jnp.concatenate(
            [jnp.where(group == g, value, zero) for g in range(high)], axis=0
        )
        part = dot(picked, hot, NT)
        col = col_ref[...]
        half = iota((2 * high, block), 0)
        digit = jnp.where((half & 1) == 0, col >> 5, col & 31)
        digits = jnp.where((half >> 1) == group, digit, 0).astype(F32).astype(BF)
        cpart = dot(digits, hot, NT)

        @pl.when(step == 0)
        def _():
            acc_ref[...] = part
            cacc_ref[...] = cpart

        @pl.when(step > 0)
        def _():
            acc_ref[...] += part
            cacc_ref[...] += cpart

        @pl.when(step == steps - 1)
        def _():
            for o in range(npatch):
                g, b = o // low, o % low
                cut = slice(b * bucket, (b + 1) * bucket)
                out_ref[o, :rows, :] = acc_ref[g * rows : (g + 1) * rows, cut].astype(BF)
                out_ref[o, rows : rows + 2, :] = cacc_ref[2 * g : 2 * g + 2, cut].astype(BF)

    lane = pl.BlockSpec((1, block), lambda i: (0, i))
    return pl.pallas_call(
        kernel,
        grid=(steps,),
        out_shape=jax.ShapeDtypeStruct((npatch, rows + 2, bucket), BF),
        in_specs=[pl.BlockSpec((width, block), lambda i: (0, i))] + [lane] * 4,
        out_specs=pl.BlockSpec((npatch, rows + 2, bucket), lambda i: (0, 0, 0)),
        scratch_shapes=[
            pltpu.VMEM((high * rows, low * bucket), F32),
            pltpu.VMEM((2 * high, low * bucket), F32),
        ],
        compiler_params=params(60),
        name="bucket_tiles",
    )(land_rows, weight, owners, ranks, columns)


def lane_swap(rows, a, b):
    source = iota((rows, rows), 0)
    target = iota((rows, rows), 1)
    return ((source % b) * a + source // b == target).astype(F32).astype(BF)


def sort_land(pos, land_rows, levels, first):
    width, tiles = land_rows.shape
    span = tiles // PARTS
    block = 512

    def kernel(pos_ref, x_ref, low_ref, high_ref):
        swap = lane_swap(width, width // levels, levels)
        for c in range(tiles // block):
            part = c * block // span
            cut = slice(part * span, (part + 1) * span)
            place = iota((block, span), 0) + (c * block - part * span)
            hot = (place == pos_ref[:, cut]).astype(F32).astype(BF)
            moved = dot(hot, x_ref[:, cut], NT).astype(BF)
            value = dot(moved, swap).astype(BF)
            at = c * block
            if at < first:
                low_ref[at : at + block, :] = value
            else:
                high_ref[at - first : at - first + block, :] = value

    return pl.pallas_call(
        kernel,
        out_shape=(
            jax.ShapeDtypeStruct((first, width), BF),
            jax.ShapeDtypeStruct((tiles - first, width), BF),
        ),
        in_specs=[VMEM, VMEM],
        out_specs=(VMEM, VMEM),
        compiler_params=params(60),
        name="sort_land",
    )(pos, land_rows)


def screen_forecast(received, base_rows, levels, obs_column, copies):
    npatch, rows2, _ = received.shape
    rows = rows2 - 2
    nobs = obs_column.shape[0]
    width, columns = base_rows.shape
    group = 8

    def kernel(in_ref, base_ref, obs_ref, out_ref):
        obs = obs_ref[...]
        place = iota((nobs, columns), 1)
        surface = (iota((rows, width), 0) * levels == iota((rows, width), 1)).astype(F32)
        base = dot(surface.astype(BF), base_ref[...]).astype(BF)
        acc = dot(base, (obs == place).astype(F32).astype(BF), NT)
        for g in range(npatch // group):
            values = jnp.concatenate(
                [in_ref[g * group + i, :rows, :] for i in range(group)], axis=1
            )
            digits = jnp.concatenate(
                [in_ref[g * group + i, rows:, :] for i in range(group)], axis=1
            ).astype(F32)
            col = (digits[0:1] * 32.0 + digits[1:2]).astype(I32)
            acc = acc + dot(values, (obs == col).astype(F32).astype(BF), NT)
        value = acc.astype(BF)
        for m in range(copies):
            out_ref[m] = value

    return pl.pallas_call(
        kernel,
        out_shape=jax.ShapeDtypeStruct((copies, rows, nobs), BF),
        in_specs=[VMEM, VMEM, VMEM],
        out_specs=VMEM,
        compiler_params=params(24),
        name="screen_forecast",
    )(received, base_rows, obs_column)


def mix_land(pieces, sources, starts, mixes, pos, land_rows, mask_row, levels):
    slots = len(pieces)
    flat = [piece for group in pieces for piece in group]
    places = [
        (s, sum(p.shape[0] for p in group[:i]))
        for s, group in enumerate(pieces)
        for i in range(len(group))
    ]
    width, tiles = land_rows.shape
    local = width // levels
    npatch = mixes.shape[0]
    members = mixes.shape[2]
    span = tiles // PARTS
    window = 48
    lanes = 128
    count = len(flat)

    def kernel(src_ref, start_ref, *refs):
        piece_refs = refs[:count]
        mix_ref, pos_ref, land_ref, mask_ref, out_ref = refs[count : count + 5]
        state_ref, tiled_ref, y_ref, sems = refs[count + 5 :]
        step = pl.program_id(0)

        @pl.when(step == 0)
        def _():
            copies = [
                pltpu.make_async_copy(
                    piece_refs[i],
                    state_ref.at[s, pl.ds(at, piece_refs[i].shape[0]), :],
                    sems.at[i],
                )
                for i, (s, at) in enumerate(places)
            ]
            for copy in copies:
                copy.start()
            for s in range(slots):
                spread = (
                    iota((members, lanes), 0)
                    == (iota((members, lanes), 1) & (local - 1)) + src_ref[s] * local
                )
                tiled_ref[:, s * lanes : (s + 1) * lanes] = dot(
                    mix_ref[...], spread.astype(F32).astype(BF)
                ).astype(BF)
            lane_level = iota((local, lanes), 1) // local
            y_ref[...] = jnp.zeros_like(y_ref)
            for copy in copies:
                copy.wait()

            def weight_of(o, s):
                at = pl.multiple_of(o * local, local)
                parts = []
                for t in (s, s + 1):
                    small = tiled_ref[pl.ds(at, local), t * lanes : (t + 1) * lanes]
                    zero = jnp.zeros_like(small)
                    parts += [
                        jnp.where(lane_level == l, small, zero) for l in range(lanes // local)
                    ]
                return jnp.concatenate(parts, axis=0)

            def mixed(o, cuts):
                acc = None
                for s in range(0, slots, 2):
                    rows = [
                        jnp.concatenate(
                            [
                                state_ref[t, pl.ds(at, window), h * lanes : (h + 1) * lanes]
                                for t in (s, s + 1)
                            ],
                            axis=1,
                        )
                        for h in range(width // lanes)
                        for at in cuts
                    ]
                    part = dot(jnp.concatenate(rows, axis=0), weight_of(o, s))
                    acc = part if acc is None else acc + part
                half = len(cuts) * window
                return jnp.concatenate(
                    [acc[h * half : (h + 1) * half] for h in range(width // lanes)], axis=1
                ).astype(BF)

            def put(part, base, first, end, value):
                at = pl.multiple_of(part * span + base, 16)
                row = iota((window, width), 0) + base
                keep = row >= first
                if end is not None:
                    keep = jnp.logical_and(keep, row < end)
                old = y_ref[pl.ds(at, window), :]
                y_ref[pl.ds(at, window), :] = jnp.where(keep, value, old)

            def begin(first):
                return pl.multiple_of(jnp.minimum((first // 16) * 16, span - window), 16)

            def bounds(o):
                firsts = [start_ref[o, q] for q in range(PARTS)]
                after = jnp.minimum(o + 1, npatch - 1)
                ends = [
                    jnp.where(o == npatch - 1, span, start_ref[after, q]) for q in range(PARTS)
                ]
                return firsts, ends, [begin(first) for first in firsts]

            def owners(i, unused):
                group = [i * UNROLL + u for u in range(UNROLL)]
                limits = [bounds(o) for o in group]
                values = [
                    mixed(o, [pl.multiple_of(q * span + bases[q], 16) for q in range(PARTS)])
                    for o, (firsts, ends, bases) in zip(group, limits)
                ]
                for value, (firsts, ends, bases) in zip(values, limits):
                    for q in range(PARTS):
                        put(q, bases[q], firsts[q], None, value[q * window : (q + 1) * window])
                most = 0
                for firsts, ends, bases in limits:
                    for q in range(PARTS):
                        most = jnp.maximum(most, ends[q] - bases[q] - window)

                @pl.when(most > 0)
                def _():
                    for o, (firsts, ends, bases) in zip(group, limits):
                        for q in range(PARTS):

                            def more(n, unused, o=o, q=q, first=firsts[q], end=ends[q], low=bases[q]):
                                base = begin(low + (n + 1) * window)
                                at = pl.multiple_of(q * span + base, 16)
                                put(q, base, first, end, mixed(o, [at]))
                                return unused

                            lack = jnp.maximum(ends[q] - bases[q] - window, 0)
                            lax.fori_loop(0, (lack + window - 1) // window, more, 0)

                return unused

            lax.fori_loop(0, npatch // UNROLL, owners, 0)

        hot = (iota((span, span), 0) == pos_ref[...]).astype(F32).astype(BF)
        rows = y_ref[pl.ds(pl.multiple_of(step * span, span), span), :]
        turned = dot(lane_swap(width, local, levels), rows, NT).astype(BF)
        back = dot(turned, hot).astype(BF)
        out_ref[...] = jnp.where(mask_ref[...] == 1, back, land_ref[...])

    return pl.pallas_call(
        kernel,
        grid=(PARTS,),
        out_shape=jax.ShapeDtypeStruct((width, tiles), BF),
        in_specs=[SMEM, SMEM]
        + [pl.BlockSpec(memory_space=pl.ANY)] * count
        + [
            VMEM,
            pl.BlockSpec((1, span), lambda i: (0, i)),
            pl.BlockSpec((width, span), lambda i: (0, i)),
            pl.BlockSpec((1, span), lambda i: (0, i)),
        ],
        out_specs=pl.BlockSpec((width, span), lambda i: (0, i)),
        scratch_shapes=[
            pltpu.VMEM((slots, tiles, width), BF),
            pltpu.VMEM((npatch * local, slots * lanes), BF),
            pltpu.VMEM((tiles, width), BF),
            pltpu.SemaphoreType.DMA((count,)),
        ],
        compiler_params=params(60),
        name="mix_land",
    )(
        sources,
        starts,
        *flat,
        mixes.reshape(npatch * local, members),
        pos,
        land_rows,
        mask_row,
    )


def exact(a, b, dims=NN):
    return lax.dot_general(a, b, dims, precision=PRECISE, preferred_element_type=F32)


def screen_stats(ensemble, obs_value, obs_error):
    count, local, nobs = ensemble.shape
    members = count * local
    half = members // 2

    def kernel(in_ref, value_ref, error_ref, out_ref):
        rows = jnp.concatenate([in_ref[m].astype(F32) for m in range(count)], axis=0)
        center = jnp.mean(rows, axis=0, keepdims=True)
        inverse_sd = lax.rsqrt(error_ref[...])
        scaled = (rows - center) * inverse_sd
        innovation = (value_ref[...] - center) * inverse_sd
        gram = exact(scaled, scaled, NT)
        proj = exact(jnp.broadcast_to(innovation, (8, nobs)), scaled, NT)
        row, lane = iota((half, members), 0), iota((half, members), 1)
        top = gram[:half]
        from_low = jnp.logical_and(lane < half, lane >= row)
        out_ref[:half, :] = jnp.where(from_low, pltpu.roll(gram[half:], half, 1), top)
        diag = jnp.sum(jnp.where(row == lane, top, 0.0), axis=0, keepdims=True)
        tail = iota((8, members), 0)
        out_ref[half:, :] = jnp.where(tail == 0, diag, jnp.where(tail == 1, proj, 0.0))

    return pl.pallas_call(
        kernel,
        out_shape=jax.ShapeDtypeStruct((half + 8, members), F32),
        in_specs=[VMEM, VMEM, VMEM],
        out_specs=VMEM,
        compiler_params=params(16),
        name="screen_stats",
    )(ensemble, obs_value, obs_error)


def settle(own, near, listed, places, local, npatch):
    members = own.shape[1]
    half = members // 2
    count = members // local
    names = listed.shape[1]

    def kernel(list_ref, place_ref, own_ref, *refs):
        near_refs = refs[: len(near)]
        cols_ref, out_ref, hold_ref = refs[len(near) :]
        total = own_ref[...]
        for d in range(len(near)):
            used = 0
            for i in range(names):
                used = used + jnp.where(list_ref[0, i] == place_ref[d], 1, 0)
            total = total + used.astype(F32) * near_refs[d][...]
        packed = total[:half]
        row, lane = iota((half, members), 0), iota((half, members), 1)
        left = lane < half
        upper = jnp.logical_and(left, lane >= row)
        strict = jnp.logical_and(left, lane > row)
        top = jnp.where(upper, 0.0, packed)
        low = pltpu.roll(jnp.where(strict, packed, 0.0), half, 1)
        sides = jnp.concatenate([top, low], axis=0)
        on_diag = jnp.where(jnp.logical_and(left, lane == row), packed, 0.0)
        top_diag = jnp.where(row == lane, total[half : half + 1], 0.0)
        diag = jnp.concatenate([top_diag, pltpu.roll(on_diag, half, 1)], axis=0)
        eye = (iota((members, members), 0) == iota((members, members), 1)).astype(F32)
        system = sides + sides.T + diag + (members - 1.0) * eye
        scale = jnp.sum(jnp.sum(system * eye, axis=1, keepdims=True), axis=0, keepdims=True)
        upper_iter = system / scale
        middle = 1.5 * eye - 0.5 * upper_iter
        upper_iter = exact(upper_iter, middle)
        lower_iter = middle
        for step in range(SWEEPS - 1):
            middle = 1.5 * eye - 0.5 * exact(lower_iter, upper_iter)
            if step < SWEEPS - 2:
                upper_iter = exact(upper_iter, middle)
            lower_iter = exact(middle, lower_iter)
        inv_root = lower_iter * lax.rsqrt(scale)
        proj = jnp.broadcast_to(total[half + 1 : half + 2], (8, members))
        shift = exact(exact(proj, inv_root, NT), inv_root, NT)[:1]
        spread = shift + math.sqrt(members - 1.0) * inv_root
        hold_ref[...] = spread - jnp.mean(spread, axis=1, keepdims=True) + 1.0 / members
        mine = hold_ref[pl.ds(pl.multiple_of(place_ref[len(near)] * local, local), local), :]
        cols_ref[...] = mine.astype(BF)
        flipped = mine.T
        blocks = jnp.concatenate(
            [flipped[m * local : (m + 1) * local] for m in range(count)], axis=1
        ).astype(BF)
        for p in range(npatch):
            out_ref[p] = blocks

    return pl.pallas_call(
        kernel,
        out_shape=(
            jax.ShapeDtypeStruct((local, members), BF),
            jax.ShapeDtypeStruct((npatch, local, members), BF),
        ),
        in_specs=[SMEM, SMEM] + [VMEM] * (1 + len(near)),
        out_specs=(VMEM, VMEM),
        scratch_shapes=[pltpu.VMEM((members, members), F32)],
        compiler_params=params(16),
        name="settle",
    )(listed, places, own, *near)


def analysis(
    atmos,
    land,
    land_mask,
    tile_owner,
    tile_column,
    tile_weight,
    obs_value,
    observation_column,
    obs_error,
    loc_blocks,
):
    barrier = lax.optimization_barrier
    npatch = lax.axis_size("patch")
    mem_count = lax.axis_size("mem")
    local, levels, columns = atmos.shape
    layers, tiles = (land.shape[1], land.shape[2])
    bucket = 2 * tiles // npatch
    row_width = max(2, npatch // 8)
    first = 3 * tiles // 8
    mem_rank = lax.axis_index("mem")
    patch_rank = lax.axis_index("patch")

    atmos_rows = atmos.reshape(local * levels, columns)
    atmos_parts = [shifted(atmos_rows, "mem", s) for s in (1, -1, 2)]

    owners = tile_owner.reshape(1, tiles)
    land_rows = land.reshape(local * layers, tiles)
    mask_row = land_mask.reshape(1, tiles)
    ranks, pos, starts = order_tiles(owners, npatch)
    packed = bucket_tiles(
        land_rows,
        layers,
        (tile_weight.astype(F32) * land_mask.astype(F32)).reshape(1, tiles),
        owners,
        ranks,
        tile_column.reshape(1, tiles),
        npatch,
        bucket,
    )
    received = lax.all_to_all(packed, "patch", split_axis=0, concat_axis=0, tiled=True)

    low, high = sort_land(pos, land_rows, layers, first)
    low_prev = shifted(low, "mem", 1)
    low_next = shifted(low, "mem", -1)

    forecast = screen_forecast(
        received, atmos_rows, levels, observation_column.reshape(-1, 1), mem_count
    )
    forecast, low_prev, low_next = barrier((forecast, low_prev, low_next))
    ensemble = lax.all_to_all(forecast, "mem", split_axis=0, concat_axis=0, tiled=True)
    ensemble, high, low_prev, low_next = barrier((ensemble, high, low_prev, low_next))
    high_prev = shifted(high, "mem", 1)
    high_next = shifted(high, "mem", -1)
    low_far = [
        shifted(low_prev[: first // 2], "mem", 1), shifted(low_next[first // 2 :], "mem", -1)
    ]

    own_stats = screen_stats(ensemble, obs_value.reshape(1, -1), obs_error.reshape(1, -1))
    offsets = (row_width, -row_width, 1, -1)
    near = [shifted(own_stats, "patch", o) for o in offsets]
    places = [(patch_rank - o) % npatch for o in offsets]
    places = jnp.stack(places + [mem_rank]).astype(I32)
    own_cols, mixes = settle(own_stats, near, loc_blocks, places, local, npatch)
    all_mixes = lax.all_to_all(mixes, "patch", split_axis=0, concat_axis=0, tiled=True)
    own_cols, high_prev, high_next = barrier((own_cols, high_prev, high_next))
    split = high.shape[0] // 2
    high_far = [shifted(high_prev[:split], "mem", 1), shifted(high_next[split:], "mem", -1)]

    slot_source = [mem_rank, mem_rank - 1, mem_rank + 1, mem_rank - 2]
    sources = jnp.stack([s % mem_count for s in slot_source]).astype(I32)
    atmos_out = 0.0
    for part, source in zip([atmos_rows] + atmos_parts, slot_source):
        rows = lax.dynamic_slice_in_dim(own_cols, (source % mem_count) * local, local, 1)
        atmos_out = atmos_out + jnp.einsum(
            "jk,klc->jlc", rows, part.reshape(local, levels, columns), preferred_element_type=F32
        )
    atmos_analysis = atmos_out.astype(BF)

    land_out = mix_land(
        [[low, high], [low_prev, high_prev], [low_next, high_next], low_far + high_far],
        sources,
        starts,
        all_mixes,
        pos,
        land_rows,
        mask_row,
        layers,
    )
    return (atmos_analysis, land_out.reshape(local, layers, tiles))


def solution(mesh):
    in_specs = (
        P("mem", None, "patch"),
        P("mem", None, "patch"),
        P("patch"),
        P("patch", None),
        P("patch"),
        P("patch"),
        P("patch"),
        P("patch"),
        P("patch"),
        P("patch", None),
    )
    out_specs = (P("mem", None, "patch"), P("mem", None, "patch"))
    return jax.shard_map(
        analysis, mesh=mesh, in_specs=in_specs, out_specs=out_specs, check_vma=False
    )
```

```python
import math

import jax
import jax.numpy as jnp
from jax import lax
from jax.experimental import pallas as pl
from jax.experimental.pallas import tpu as pltpu
from jax.sharding import PartitionSpec as P

SWEEPS = 10
PRECISE = lax.Precision.HIGHEST
BF = jnp.bfloat16
F32 = jnp.float32
I32 = jnp.int32

NN = (((1,), (0,)), ((), ()))
NT = (((1,), (1,)), ((), ()))


def dot(a, b, dims=NN):
    return lax.dot_general(a, b, dims, preferred_element_type=F32)


def iota(shape, axis):
    return lax.broadcasted_iota(I32, shape, axis)


VMEM = pl.BlockSpec(memory_space=pltpu.VMEM)
SMEM = pl.BlockSpec(memory_space=pltpu.SMEM)


def params(mib):
    return pltpu.CompilerParams(vmem_limit_bytes=mib * 1024 * 1024)


def shifted(value, axis, steps):
    count = lax.axis_size(axis)
    pairs = [(source, (source + steps) % count) for source in range(count)]
    return lax.ppermute(value, axis, pairs)


PARTS = 4
UNROLL = 4


def order_tiles(owners, npatch):
    tiles = owners.shape[1]
    block = 512
    per_part = tiles // PARTS // block

    def kernel(owner_ref, rank_ref, pos_ref, start_ref):
        before = (iota((block, block), 0) < iota((block, block), 1)).astype(BF)
        lower = (iota((npatch, npatch), 0) > iota((npatch, npatch), 1)).astype(BF)
        done = jnp.zeros((npatch, 1), F32)
        for part in range(PARTS):
            carry = jnp.zeros((npatch, 1), F32)
            held = []
            for c in range(per_part):
                at = (part * per_part + c) * block
                hot = owner_ref[:, at : at + block] == iota((npatch, block), 0)
                ahead = dot(hot.astype(BF), before) + carry
                hot = hot.astype(F32)
                carry = carry + jnp.sum(hot, axis=1, keepdims=True)
                held.append((at, hot, ahead))
            starts = dot(lower, jnp.broadcast_to(carry, (npatch, 128)).astype(BF))[:, :1]
            start_ref[:, part : part + 1] = starts.astype(I32)
            for at, hot, ahead in held:
                rank = jnp.sum(hot * (ahead + done), axis=0, keepdims=True)
                pos = jnp.sum(hot * (ahead + starts), axis=0, keepdims=True)
                rank_ref[:, at : at + block] = rank.astype(I32)
                pos_ref[:, at : at + block] = pos.astype(I32)
            done = done + carry
        start_ref[:, PARTS:] = jnp.zeros((npatch, PARTS), I32)

    return pl.pallas_call(
        kernel,
        out_shape=(
            jax.ShapeDtypeStruct((1, tiles), I32),
            jax.ShapeDtypeStruct((1, tiles), I32),
            jax.ShapeDtypeStruct((npatch, 2 * PARTS), I32),
        ),
        in_specs=[VMEM],
        out_specs=(VMEM, VMEM, VMEM),
        compiler_params=params(60),
        name="order_tiles",
    )(owners)


def bucket_tiles(land_rows, levels, weight, owners, ranks, columns, npatch, bucket):
    width, tiles = land_rows.shape
    rows = width // levels
    low = 4
    high = npatch // low
    block = 1024
    steps = tiles // block

    def kernel(
        x_ref, weight_ref, owner_ref, rank_ref, col_ref, out_ref, acc_ref, cacc_ref
    ):
        step = pl.program_id(0)
        owner = owner_ref[...]
        slot = (owner & (low - 1)) * bucket + rank_ref[...]
        hot = (iota((low * bucket, block), 0) == slot).astype(F32).astype(BF)
        group = owner >> 2
        surface = (iota((rows, width), 0) * levels == iota((rows, width), 1)).astype(F32)
        value = (dot(surface.astype(BF), x_ref[...]) * weight_ref[...]).astype(BF)
        zero = jnp.zeros_like(value)
        picked = jnp.concatenate(
            [jnp.where(group == g, value, zero) for g in range(high)], axis=0
        )
        part = dot(picked, hot, NT)
        col = col_ref[...]
        half = iota((2 * high, block), 0)
        digit = jnp.where((half & 1) == 0, col >> 5, col & 31)
        digits = jnp.where((half >> 1) == group, digit, 0).astype(F32).astype(BF)
        cpart = dot(digits, hot, NT)

        @pl.when(step == 0)
        def _():
            acc_ref[...] = part
            cacc_ref[...] = cpart

        @pl.when(step > 0)
        def _():
            acc_ref[...] += part
            cacc_ref[...] += cpart

        @pl.when(step == steps - 1)
        def _():
            for o in range(npatch):
                g, b = o // low, o % low
                cut = slice(b * bucket, (b + 1) * bucket)
                out_ref[o, :rows, :] = acc_ref[g * rows : (g + 1) * rows, cut].astype(BF)
                out_ref[o, rows : rows + 2, :] = cacc_ref[2 * g : 2 * g + 2, cut].astype(BF)

    lane = pl.BlockSpec((1, block), lambda i: (0, i))
    return pl.pallas_call(
        kernel,
        grid=(steps,),
        out_shape=jax.ShapeDtypeStruct((npatch, rows + 2, bucket), BF),
        in_specs=[pl.BlockSpec((width, block), lambda i: (0, i))] + [lane] * 4,
        out_specs=pl.BlockSpec((npatch, rows + 2, bucket), lambda i: (0, 0, 0)),
        scratch_shapes=[
            pltpu.VMEM((high * rows, low * bucket), F32),
            pltpu.VMEM((2 * high, low * bucket), F32),
        ],
        compiler_params=params(60),
        name="bucket_tiles",
    )(land_rows, weight, owners, ranks, columns)


def lane_swap(rows, a, b):
    source = iota((rows, rows), 0)
    target = iota((rows, rows), 1)
    return ((source % b) * a + source // b == target).astype(F32).astype(BF)


def sort_land(pos, land_rows, levels, skip, shares):
    width, tiles = land_rows.shape
    span = tiles // PARTS
    block = 512
    whole = [sum(shares[:i]) * span for i in range(len(shares))]

    def kernel(pos_ref, x_ref, *out_refs):
        swap = lane_swap(width, width // levels, levels)
        for out_ref, begin in zip(out_refs, whole):
            for at in range(0, out_ref.shape[0], block):
                part = (begin + at) // span
                cut = slice((skip + part) * span, (skip + part + 1) * span)
                place = iota((block, span), 0) + (begin + at - part * span)
                hot = (place == pos_ref[:, cut]).astype(F32).astype(BF)
                moved = dot(hot, x_ref[:, (cut.start - low) : (cut.stop - low)], NT).astype(BF)
                out_ref[at : at + block, :] = dot(moved, swap).astype(BF)

    count = sum(shares)
    low = skip * span if skip == 0 else 0
    taken = (
        pl.BlockSpec((width, count * span), lambda i: (0, 0))
        if skip == 0
        else pl.BlockSpec((width, tiles), lambda i: (0, 0))
    )
    return pl.pallas_call(
        kernel,
        grid=(1,),
        out_shape=[jax.ShapeDtypeStruct((n * span, width), BF) for n in shares],
        in_specs=[pl.BlockSpec((1, tiles), lambda i: (0, 0)), taken],
        out_specs=[pl.BlockSpec((n * span, width), lambda i: (0, 0)) for n in shares],
        compiler_params=params(60),
        name="sort_land",
    )(pos, land_rows)


def screen_forecast(received, base_rows, levels, obs_column, copies):
    npatch, rows2, _ = received.shape
    rows = rows2 - 2
    nobs = obs_column.shape[0]
    width, columns = base_rows.shape
    group = 8

    def kernel(in_ref, base_ref, obs_ref, out_ref):
        obs = obs_ref[...]
        place = iota((nobs, columns), 1)
        surface = (iota((rows, width), 0) * levels == iota((rows, width), 1)).astype(F32)
        base = dot(surface.astype(BF), base_ref[...]).astype(BF)
        acc = dot(base, (obs == place).astype(F32).astype(BF), NT)
        for g in range(npatch // group):
            values = jnp.concatenate(
                [in_ref[g * group + i, :rows, :] for i in range(group)], axis=1
            )
            digits = jnp.concatenate(
                [in_ref[g * group + i, rows:, :] for i in range(group)], axis=1
            ).astype(F32)
            col = (digits[0:1] * 32.0 + digits[1:2]).astype(I32)
            acc = acc + dot(values, (obs == col).astype(F32).astype(BF), NT)
        value = acc.astype(BF)
        for m in range(copies):
            out_ref[m] = value

    return pl.pallas_call(
        kernel,
        out_shape=jax.ShapeDtypeStruct((copies, rows, nobs), BF),
        in_specs=[VMEM, VMEM, VMEM],
        out_specs=VMEM,
        compiler_params=params(24),
        name="screen_forecast",
    )(received, base_rows, obs_column)


def mix_land(pieces, ids, starts, mixes, pos, land_rows, mask_row, levels):
    slots = len(pieces)
    flat = [piece for group in pieces for piece in group]
    places = [
        (s, sum(p.shape[0] for p in group[:i]))
        for s, group in enumerate(pieces)
        for i in range(len(group))
    ]
    width, tiles = land_rows.shape
    local = width // levels
    npatch = mixes.shape[0]
    members = mixes.shape[2]
    span = tiles // PARTS
    window = 48
    lanes = 128
    count = len(flat)

    def kernel(id_ref, start_ref, *refs):
        piece_refs = refs[:count]
        mix_ref, pos_ref, land_ref, mask_ref, out_ref = refs[count : count + 5]
        state_ref, tiled_ref, y_ref, sems = refs[count + 5 :]
        step = pl.program_id(0)

        @pl.when(step == 0)
        def _():
            copies = [
                pltpu.make_async_copy(
                    piece_refs[i],
                    state_ref.at[s, pl.ds(at, piece_refs[i].shape[0]), :],
                    sems.at[i],
                )
                for i, (s, at) in enumerate(places)
            ]
            for copy in copies:
                copy.start()
            for s in range(slots):
                spread = (
                    iota((members, lanes), 0)
                    == (iota((members, lanes), 1) & (local - 1)) + (id_ref[1] + (0, slots - 1, 1, 2)[s]) % slots * local
                )
                tiled_ref[:, s * lanes : (s + 1) * lanes] = dot(
                    mix_ref[...], spread.astype(F32).astype(BF)
                ).astype(BF)
            lane_level = iota((local, lanes), 1) // local
            y_ref[...] = jnp.zeros_like(y_ref)
            for copy in copies:
                copy.wait()

            def weight_of(o, s):
                at = pl.multiple_of(o * local, local)
                parts = []
                for t in (s, s + 1):
                    small = tiled_ref[pl.ds(at, local), t * lanes : (t + 1) * lanes]
                    zero = jnp.zeros_like(small)
                    parts += [
                        jnp.where(lane_level == l, small, zero) for l in range(lanes // local)
                    ]
                return jnp.concatenate(parts, axis=0)

            def mixed(o, cuts):
                acc = None
                for s in range(0, slots, 2):
                    rows = [
                        jnp.concatenate(
                            [
                                state_ref[t, pl.ds(at, window), h * lanes : (h + 1) * lanes]
                                for t in (s, s + 1)
                            ],
                            axis=1,
                        )
                        for h in range(width // lanes)
                        for at in cuts
                    ]
                    part = dot(jnp.concatenate(rows, axis=0), weight_of(o, s))
                    acc = part if acc is None else acc + part
                half = len(cuts) * window
                return jnp.concatenate(
                    [acc[h * half : (h + 1) * half] for h in range(width // lanes)], axis=1
                ).astype(BF)

            def put(part, base, first, end, value):
                at = pl.multiple_of(part * span + base, 16)
                row = iota((window, width), 0) + base
                keep = row >= first
                if end is not None:
                    keep = jnp.logical_and(keep, row < end)
                old = y_ref[pl.ds(at, window), :]
                y_ref[pl.ds(at, window), :] = jnp.where(keep, value, old)

            def begin(first):
                return pl.multiple_of(jnp.minimum((first // 16) * 16, span - window), 16)

            def bounds(o):
                firsts = [start_ref[o, q] for q in range(PARTS)]
                after = jnp.minimum(o + 1, npatch - 1)
                ends = [
                    jnp.where(o == npatch - 1, span, start_ref[after, q]) for q in range(PARTS)
                ]
                return firsts, ends, [begin(first) for first in firsts]

            def owners(i, unused):
                group = [i * UNROLL + u for u in range(UNROLL)]
                limits = [bounds(o) for o in group]
                values = [
                    mixed(o, [pl.multiple_of(q * span + bases[q], 16) for q in range(PARTS)])
                    for o, (firsts, ends, bases) in zip(group, limits)
                ]
                for value, (firsts, ends, bases) in zip(values, limits):
                    for q in range(PARTS):
                        put(q, bases[q], firsts[q], None, value[q * window : (q + 1) * window])
                most = 0
                for firsts, ends, bases in limits:
                    for q in range(PARTS):
                        most = jnp.maximum(most, ends[q] - bases[q] - window)

                @pl.when(most > 0)
                def _():
                    for o, (firsts, ends, bases) in zip(group, limits):
                        for q in range(PARTS):

                            def more(n, unused, o=o, q=q, first=firsts[q], end=ends[q], low=bases[q]):
                                base = begin(low + (n + 1) * window)
                                at = pl.multiple_of(q * span + base, 16)
                                put(q, base, first, end, mixed(o, [at]))
                                return unused

                            lack = jnp.maximum(ends[q] - bases[q] - window, 0)
                            lax.fori_loop(0, (lack + window - 1) // window, more, 0)

                return unused

            lax.fori_loop(0, npatch // UNROLL, owners, 0)

        hot = (iota((span, span), 0) == pos_ref[...]).astype(F32).astype(BF)
        rows = y_ref[pl.ds(pl.multiple_of(step * span, span), span), :]
        turned = dot(lane_swap(width, local, levels), rows, NT).astype(BF)
        back = dot(turned, hot).astype(BF)
        out_ref[...] = jnp.where(mask_ref[...] == 1, back, land_ref[...])

    return pl.pallas_call(
        kernel,
        grid=(PARTS,),
        out_shape=jax.ShapeDtypeStruct((width, tiles), BF),
        in_specs=[SMEM, SMEM]
        + [pl.BlockSpec(memory_space=pl.ANY)] * count
        + [
            VMEM,
            pl.BlockSpec((1, span), lambda i: (0, i)),
            pl.BlockSpec((width, span), lambda i: (0, i)),
            pl.BlockSpec((1, span), lambda i: (0, i)),
        ],
        out_specs=pl.BlockSpec((width, span), lambda i: (0, i)),
        scratch_shapes=[
            pltpu.VMEM((slots, tiles, width), BF),
            pltpu.VMEM((npatch * local, slots * lanes), BF),
            pltpu.VMEM((tiles, width), BF),
            pltpu.SemaphoreType.DMA((count,)),
        ],
        compiler_params=params(60),
        name="mix_land",
    )(
        ids,
        starts,
        *flat,
        mixes.reshape(npatch * local, members),
        pos,
        land_rows,
        mask_row,
    )


def exact(a, b, dims=NN):
    return lax.dot_general(a, b, dims, precision=PRECISE, preferred_element_type=F32)


def screen_stats(ensemble, obs_value, obs_error):
    count, local, nobs = ensemble.shape
    members = count * local
    half = members // 2

    def kernel(in_ref, value_ref, error_ref, out_ref):
        rows = jnp.concatenate([in_ref[m].astype(F32) for m in range(count)], axis=0)
        center = jnp.mean(rows, axis=0, keepdims=True)
        inverse_sd = lax.rsqrt(error_ref[...])
        scaled = (rows - center) * inverse_sd
        innovation = (value_ref[...] - center) * inverse_sd
        gram = exact(scaled, scaled, NT)
        proj = exact(jnp.broadcast_to(innovation, (8, nobs)), scaled, NT)
        row, lane = iota((half, members), 0), iota((half, members), 1)
        top = gram[:half]
        from_low = jnp.logical_and(lane < half, lane >= row)
        out_ref[:half, :] = jnp.where(from_low, pltpu.roll(gram[half:], half, 1), top)
        diag = jnp.sum(jnp.where(row == lane, top, 0.0), axis=0, keepdims=True)
        tail = iota((8, members), 0)
        out_ref[half:, :] = jnp.where(tail == 0, diag, jnp.where(tail == 1, proj, 0.0))

    return pl.pallas_call(
        kernel,
        out_shape=jax.ShapeDtypeStruct((half + 8, members), F32),
        in_specs=[VMEM, VMEM, VMEM],
        out_specs=VMEM,
        compiler_params=params(16),
        name="screen_stats",
    )(ensemble, obs_value, obs_error)


def settle(own, near, listed, ids, offsets, local, npatch):
    members = own.shape[1]
    half = members // 2
    count = members // local
    names = listed.shape[1]

    def kernel(list_ref, id_ref, own_ref, *refs):
        near_refs = refs[: len(near)]
        cols_ref, out_ref, hold_ref = refs[len(near) :]
        total = own_ref[...]
        for d in range(len(near)):
            source = (id_ref[0] - offsets[d] + npatch) % npatch
            used = 0
            for i in range(names):
                used = used + jnp.where(list_ref[0, i] == source, 1, 0)
            total = total + used.astype(F32) * near_refs[d][...]
        packed = total[:half]
        row, lane = iota((half, members), 0), iota((half, members), 1)
        left = lane < half
        upper = jnp.logical_and(left, lane >= row)
        strict = jnp.logical_and(left, lane > row)
        top = jnp.where(upper, 0.0, packed)
        low = pltpu.roll(jnp.where(strict, packed, 0.0), half, 1)
        sides = jnp.concatenate([top, low], axis=0)
        on_diag = jnp.where(jnp.logical_and(left, lane == row), packed, 0.0)
        top_diag = jnp.where(row == lane, total[half : half + 1], 0.0)
        diag = jnp.concatenate([top_diag, pltpu.roll(on_diag, half, 1)], axis=0)
        eye = (iota((members, members), 0) == iota((members, members), 1)).astype(F32)
        system = sides + sides.T + diag + (members - 1.0) * eye
        scale = jnp.sum(jnp.sum(system * eye, axis=1, keepdims=True), axis=0, keepdims=True)
        upper_iter = system / scale
        middle = 1.5 * eye - 0.5 * upper_iter
        upper_iter = exact(upper_iter, middle)
        lower_iter = middle
        for step in range(SWEEPS - 1):
            middle = 1.5 * eye - 0.5 * exact(lower_iter, upper_iter)
            if step < SWEEPS - 2:
                upper_iter = exact(upper_iter, middle)
            lower_iter = exact(middle, lower_iter)
        inv_root = lower_iter * lax.rsqrt(scale)
        proj = jnp.broadcast_to(total[half + 1 : half + 2], (8, members))
        shift = exact(exact(proj, inv_root, NT), inv_root, NT)[:1]
        spread = shift + math.sqrt(members - 1.0) * inv_root
        hold_ref[...] = spread - jnp.mean(spread, axis=1, keepdims=True) + 1.0 / members
        mine = hold_ref[pl.ds(pl.multiple_of(id_ref[1] * local, local), local), :]
        cols_ref[...] = mine.astype(BF)
        flipped = mine.T
        blocks = jnp.concatenate(
            [flipped[m * local : (m + 1) * local] for m in range(count)], axis=1
        ).astype(BF)
        for p in range(npatch):
            out_ref[p] = blocks

    return pl.pallas_call(
        kernel,
        out_shape=(
            jax.ShapeDtypeStruct((local, members), BF),
            jax.ShapeDtypeStruct((npatch, local, members), BF),
        ),
        in_specs=[SMEM, SMEM] + [VMEM] * (1 + len(near)),
        out_specs=(VMEM, VMEM),
        scratch_shapes=[pltpu.VMEM((members, members), F32)],
        compiler_params=params(16),
        name="settle",
    )(listed, ids, own, *near)


def analysis(
    atmos,
    land,
    land_mask,
    tile_owner,
    tile_column,
    tile_weight,
    obs_value,
    observation_column,
    obs_error,
    loc_blocks,
):
    barrier = lax.optimization_barrier
    npatch = lax.axis_size("patch")
    mem_count = lax.axis_size("mem")
    local, levels, columns = atmos.shape
    layers, tiles = (land.shape[1], land.shape[2])
    bucket = 2 * tiles // npatch
    row_width = max(2, npatch // 8)
    mem_rank = lax.axis_index("mem")
    ids = jnp.stack([lax.axis_index("patch"), mem_rank]).astype(I32)

    atmos_rows = atmos.reshape(local * levels, columns)
    atmos_parts = [shifted(atmos_rows, "mem", s) for s in (1, -1, 2)]

    owners = tile_owner.reshape(1, tiles)
    land_rows = land.reshape(local * layers, tiles)
    mask_row = land_mask.reshape(1, tiles)
    ranks, pos, starts = order_tiles(owners, npatch)
    packed = bucket_tiles(
        land_rows,
        layers,
        (tile_weight.astype(F32) * land_mask.astype(F32)).reshape(1, tiles),
        owners,
        ranks,
        tile_column.reshape(1, tiles),
        npatch,
        bucket,
    )
    received = lax.all_to_all(packed, "patch", split_axis=0, concat_axis=0, tiled=True)

    (first,) = sort_land(pos, land_rows, layers, 0, (1,))
    first_prev = shifted(first, "mem", 1)
    first_next = shifted(first, "mem", -1)
    second, rest = sort_land(pos, land_rows, layers, 1, (1, PARTS - 2))
    second_prev = shifted(second, "mem", 1)
    second_next = shifted(second, "mem", -1)

    forecast = screen_forecast(
        received, atmos_rows, levels, observation_column.reshape(-1, 1), mem_count
    )
    forecast, first_prev, first_next, second_prev, second_next, rest = barrier(
        (forecast, first_prev, first_next, second_prev, second_next, rest)
    )
    ensemble = lax.all_to_all(forecast, "mem", split_axis=0, concat_axis=0, tiled=True)
    rest_prev = shifted(rest, "mem", 1)
    rest_next = shifted(rest, "mem", -1)
    first_far = shifted(first_prev, "mem", 1)
    second_far = shifted(second_prev, "mem", 1)

    own_stats = screen_stats(ensemble, obs_value.reshape(1, -1), obs_error.reshape(1, -1))
    offsets = (row_width, -row_width, 1, -1)
    near = [shifted(own_stats, "patch", o) for o in offsets]
    own_cols, mixes = settle(own_stats, near, loc_blocks, ids, offsets, local, npatch)
    own_cols, rest_next = barrier((own_cols, rest_next))
    rest_far = shifted(rest_next, "mem", -1)
    all_mixes = lax.all_to_all(mixes, "patch", split_axis=0, concat_axis=0, tiled=True)

    slot_source = [mem_rank, mem_rank - 1, mem_rank + 1, mem_rank - 2]
    atmos_out = 0.0
    for part, source in zip([atmos_rows] + atmos_parts, slot_source):
        rows = lax.dynamic_slice_in_dim(own_cols, (source % mem_count) * local, local, 1)
        atmos_out = atmos_out + jnp.einsum(
            "jk,klc->jlc", rows, part.reshape(local, levels, columns), preferred_element_type=F32
        )
    atmos_analysis = atmos_out.astype(BF)

    land_out = mix_land(
        [
            [first, second, rest],
            [first_prev, second_prev, rest_prev],
            [first_next, second_next, rest_next],
            [first_far, second_far, rest_far],
        ],
        ids,
        starts,
        all_mixes,
        pos,
        land_rows,
        mask_row,
        layers,
    )
    return (atmos_analysis, land_out.reshape(local, layers, tiles))


def solution(mesh):
    in_specs = (
        P("mem", None, "patch"),
        P("mem", None, "patch"),
        P("patch"),
        P("patch", None),
        P("patch"),
        P("patch"),
        P("patch"),
        P("patch"),
        P("patch"),
        P("patch", None),
    )
    out_specs = (P("mem", None, "patch"), P("mem", None, "patch"))
    return jax.shard_map(
        analysis, mesh=mesh, in_specs=in_specs, out_specs=out_specs, check_vma=False
    )
```

```python
import math

import jax
import jax.numpy as jnp
from jax import lax
from jax.experimental import pallas as pl
from jax.experimental.pallas import tpu as pltpu
from jax.sharding import PartitionSpec as P

SWEEPS = 10
PRECISE = lax.Precision.HIGHEST
BF = jnp.bfloat16
F32 = jnp.float32
I32 = jnp.int32

NN = (((1,), (0,)), ((), ()))
NT = (((1,), (1,)), ((), ()))


def dot(a, b, dims=NN):
    return lax.dot_general(a, b, dims, preferred_element_type=F32)


def iota(shape, axis):
    return lax.broadcasted_iota(I32, shape, axis)


VMEM = pl.BlockSpec(memory_space=pltpu.VMEM)
SMEM = pl.BlockSpec(memory_space=pltpu.SMEM)


def params(mib):
    return pltpu.CompilerParams(vmem_limit_bytes=mib * 1024 * 1024)


def shifted(value, axis, steps):
    count = lax.axis_size(axis)
    pairs = [(source, (source + steps) % count) for source in range(count)]
    return lax.ppermute(value, axis, pairs)


PARTS = 4
UNROLL = 4


def order_tiles(owners, npatch):
    tiles = owners.shape[1]
    block = 512
    per_part = tiles // PARTS // block

    def kernel(owner_ref, rank_ref, pos_ref, start_ref):
        before = (iota((block, block), 0) < iota((block, block), 1)).astype(BF)
        lower = (iota((npatch, npatch), 0) > iota((npatch, npatch), 1)).astype(BF)
        done = jnp.zeros((npatch, 1), F32)
        for part in range(PARTS):
            carry = jnp.zeros((npatch, 1), F32)
            held = []
            for c in range(per_part):
                at = (part * per_part + c) * block
                hot = owner_ref[:, at : at + block] == iota((npatch, block), 0)
                ahead = dot(hot.astype(BF), before) + carry
                hot = hot.astype(F32)
                carry = carry + jnp.sum(hot, axis=1, keepdims=True)
                held.append((at, hot, ahead))
            starts = dot(lower, jnp.broadcast_to(carry, (npatch, 128)).astype(BF))[:, :1]
            start_ref[:, part : part + 1] = starts.astype(I32)
            for at, hot, ahead in held:
                rank = jnp.sum(hot * (ahead + done), axis=0, keepdims=True)
                pos = jnp.sum(hot * (ahead + starts), axis=0, keepdims=True)
                rank_ref[:, at : at + block] = rank.astype(I32)
                pos_ref[:, at : at + block] = pos.astype(I32)
            done = done + carry
        start_ref[:, PARTS:] = jnp.zeros((npatch, PARTS), I32)

    return pl.pallas_call(
        kernel,
        out_shape=(
            jax.ShapeDtypeStruct((1, tiles), I32),
            jax.ShapeDtypeStruct((1, tiles), I32),
            jax.ShapeDtypeStruct((npatch, 2 * PARTS), I32),
        ),
        in_specs=[VMEM],
        out_specs=(VMEM, VMEM, VMEM),
        compiler_params=params(60),
        name="order_tiles",
    )(owners)


def bucket_tiles(land_rows, levels, weight, mask, owners, ranks, columns, npatch, bucket):
    width, tiles = land_rows.shape
    rows = width // levels
    low = 4
    high = npatch // low
    block = 1024
    steps = tiles // block

    def kernel(
        x_ref,
        weight_ref,
        mask_ref,
        owner_ref,
        rank_ref,
        col_ref,
        out_ref,
        acc_ref,
        cacc_ref,
        keep_ref,
    ):
        step = pl.program_id(0)
        owner = owner_ref[...]
        slot = (owner & (low - 1)) * bucket + rank_ref[...]
        hot = (iota((low * bucket, block), 0) == slot).astype(F32).astype(BF)
        group = owner >> 2
        surface = (iota((rows, width), 0) * levels == iota((rows, width), 1)).astype(F32)

        @pl.when(step == 0)
        def _():
            keep_ref[...] = weight_ref[...].astype(F32) * mask_ref[...].astype(F32)

        per_step = block // 128
        keep = keep_ref[pl.ds(pl.multiple_of(step * per_step, per_step), per_step), :]
        keep = jnp.concatenate([keep[c : c + 1] for c in range(per_step)], axis=1)
        value = (dot(surface.astype(BF), x_ref[...]) * keep).astype(BF)
        zero = jnp.zeros_like(value)
        picked = jnp.concatenate(
            [jnp.where(group == g, value, zero) for g in range(high)], axis=0
        )
        part = dot(picked, hot, NT)
        col = col_ref[...]
        half = iota((2 * high, block), 0)
        digit = jnp.where((half & 1) == 0, col >> 5, col & 31)
        digits = jnp.where((half >> 1) == group, digit, 0).astype(F32).astype(BF)
        cpart = dot(digits, hot, NT)

        @pl.when(step == 0)
        def _():
            acc_ref[...] = part
            cacc_ref[...] = cpart

        @pl.when(step > 0)
        def _():
            acc_ref[...] += part
            cacc_ref[...] += cpart

        @pl.when(step == steps - 1)
        def _():
            for o in range(npatch):
                g, b = o // low, o % low
                cut = slice(b * bucket, (b + 1) * bucket)
                out_ref[o, :rows, :] = acc_ref[g * rows : (g + 1) * rows, cut].astype(BF)
                out_ref[o, rows : rows + 2, :] = cacc_ref[2 * g : 2 * g + 2, cut].astype(BF)

    lane = pl.BlockSpec((1, block), lambda i: (0, i))
    return pl.pallas_call(
        kernel,
        grid=(steps,),
        out_shape=jax.ShapeDtypeStruct((npatch, rows + 2, bucket), BF),
        in_specs=[pl.BlockSpec((width, block), lambda i: (0, i)), VMEM, VMEM] + [lane] * 3,
        out_specs=pl.BlockSpec((npatch, rows + 2, bucket), lambda i: (0, 0, 0)),
        scratch_shapes=[
            pltpu.VMEM((high * rows, low * bucket), F32),
            pltpu.VMEM((2 * high, low * bucket), F32),
            pltpu.VMEM((tiles // 128, 128), F32),
        ],
        compiler_params=params(60),
        name="bucket_tiles",
    )(land_rows, weight, mask, owners, ranks, columns)


def lane_swap(rows, a, b):
    source = iota((rows, rows), 0)
    target = iota((rows, rows), 1)
    return ((source % b) * a + source // b == target).astype(F32).astype(BF)


def sort_land(pos, land_rows, levels, skip, count):
    width, tiles = land_rows.shape
    span = tiles // PARTS
    block = 512

    def kernel(pos_ref, x_ref, out_ref):
        swap = lane_swap(width, width // levels, levels)
        for at in range(0, count * span, block):
            part = at // span
            cut = slice(part * span, (part + 1) * span)
            place = iota((block, span), 0) + (at - part * span)
            hot = (place == pos_ref[:, cut]).astype(F32).astype(BF)
            moved = dot(hot, x_ref[:, cut], NT).astype(BF)
            out_ref[at : at + block, :] = dot(moved, swap).astype(BF)

    return pl.pallas_call(
        kernel,
        grid=(1,),
        out_shape=[jax.ShapeDtypeStruct((count * span, width), BF)],
        in_specs=[
            pl.BlockSpec((1, count * span), lambda i: (0, skip // count)),
            pl.BlockSpec((width, count * span), lambda i: (0, skip // count)),
        ],
        out_specs=[pl.BlockSpec((count * span, width), lambda i: (0, 0))],
        compiler_params=params(60),
        name="sort_land",
    )(pos, land_rows)


def screen_forecast(received, base_rows, levels, obs_column, copies):
    npatch, rows2, _ = received.shape
    rows = rows2 - 2
    nobs = obs_column.shape[0]
    width, columns = base_rows.shape
    group = 8

    def kernel(in_ref, base_ref, obs_ref, out_ref):
        obs = obs_ref[...]
        place = iota((nobs, columns), 1)
        surface = (iota((rows, width), 0) * levels == iota((rows, width), 1)).astype(F32)
        base = dot(surface.astype(BF), base_ref[...]).astype(BF)
        acc = dot(base, (obs == place).astype(F32).astype(BF), NT)
        for g in range(npatch // group):
            values = jnp.concatenate(
                [in_ref[g * group + i, :rows, :] for i in range(group)], axis=1
            )
            digits = jnp.concatenate(
                [in_ref[g * group + i, rows:, :] for i in range(group)], axis=1
            ).astype(F32)
            col = (digits[0:1] * 32.0 + digits[1:2]).astype(I32)
            acc = acc + dot(values, (obs == col).astype(F32).astype(BF), NT)
        value = acc.astype(BF)
        for m in range(copies):
            out_ref[m] = value

    return pl.pallas_call(
        kernel,
        out_shape=jax.ShapeDtypeStruct((copies, rows, nobs), BF),
        in_specs=[VMEM, VMEM, VMEM],
        out_specs=VMEM,
        compiler_params=params(24),
        name="screen_forecast",
    )(received, base_rows, obs_column)


def mix_land(pieces, ids, starts, mixes, pos, land_rows, mask_row, levels):
    slots = len(pieces)
    flat = [piece for group in pieces for piece in group]
    places = [
        (s, sum(p.shape[0] for p in group[:i]))
        for s, group in enumerate(pieces)
        for i in range(len(group))
    ]
    width, tiles = land_rows.shape
    local = width // levels
    npatch = mixes.shape[0]
    members = mixes.shape[2]
    span = tiles // PARTS
    window = 48
    lanes = 128
    count = len(flat)

    def kernel(id_ref, start_ref, *refs):
        piece_refs = refs[:count]
        mix_ref, pos_ref, land_ref, mask_ref, out_ref = refs[count : count + 5]
        state_ref, tiled_ref, y_ref, sems = refs[count + 5 :]
        step = pl.program_id(0)

        @pl.when(step == 0)
        def _():
            copies = [
                pltpu.make_async_copy(
                    piece_refs[i],
                    state_ref.at[s, pl.ds(at, piece_refs[i].shape[0]), :],
                    sems.at[i],
                )
                for i, (s, at) in enumerate(places)
            ]
            for copy in copies:
                copy.start()
            for s in range(slots):
                spread = (
                    iota((members, lanes), 0)
                    == (iota((members, lanes), 1) & (local - 1)) + (id_ref[1] + (0, slots - 1, 1, 2)[s]) % slots * local
                )
                tiled_ref[:, s * lanes : (s + 1) * lanes] = dot(
                    mix_ref[...], spread.astype(F32).astype(BF)
                ).astype(BF)
            lane_level = iota((local, lanes), 1) // local
            for copy in copies:
                copy.wait()

            def weight_of(o, s):
                at = pl.multiple_of(o * local, local)
                parts = []
                for t in (s, s + 1):
                    small = tiled_ref[pl.ds(at, local), t * lanes : (t + 1) * lanes]
                    zero = jnp.zeros_like(small)
                    parts += [
                        jnp.where(lane_level == l, small, zero) for l in range(lanes // local)
                    ]
                return jnp.concatenate(parts, axis=0)

            def mixed(o, cuts):
                acc = None
                for s in range(0, slots, 2):
                    rows = [
                        jnp.concatenate(
                            [
                                state_ref[t, pl.ds(at, window), h * lanes : (h + 1) * lanes]
                                for t in (s, s + 1)
                            ],
                            axis=1,
                        )
                        for h in range(width // lanes)
                        for at in cuts
                    ]
                    part = dot(jnp.concatenate(rows, axis=0), weight_of(o, s))
                    acc = part if acc is None else acc + part
                half = len(cuts) * window
                return jnp.concatenate(
                    [acc[h * half : (h + 1) * half] for h in range(width // lanes)], axis=1
                ).astype(BF)

            def put(part, base, first, end, value):
                at = pl.multiple_of(part * span + base, 16)
                row = iota((window, width), 0) + base
                keep = row >= first
                if end is not None:
                    keep = jnp.logical_and(keep, row < end)
                old = y_ref[pl.ds(at, window), :]
                y_ref[pl.ds(at, window), :] = jnp.where(keep, value, old)

            def begin(first):
                return pl.multiple_of(jnp.minimum((first // 16) * 16, span - window), 16)

            def bounds(o):
                firsts = [start_ref[o, q] for q in range(PARTS)]
                after = jnp.minimum(o + 1, npatch - 1)
                ends = [
                    jnp.where(o == npatch - 1, span, start_ref[after, q]) for q in range(PARTS)
                ]
                return firsts, ends, [begin(first) for first in firsts]

            def owners(i, unused):
                group = [i * UNROLL + u for u in range(UNROLL)]
                limits = [bounds(o) for o in group]
                values = [
                    mixed(o, [pl.multiple_of(q * span + bases[q], 16) for q in range(PARTS)])
                    for o, (firsts, ends, bases) in zip(group, limits)
                ]
                for value, (firsts, ends, bases) in zip(values, limits):
                    for q in range(PARTS):
                        put(q, bases[q], firsts[q], None, value[q * window : (q + 1) * window])
                most = 0
                for firsts, ends, bases in limits:
                    for q in range(PARTS):
                        most = jnp.maximum(most, ends[q] - bases[q] - window)

                @pl.when(most > 0)
                def _():
                    for o, (firsts, ends, bases) in zip(group, limits):
                        for q in range(PARTS):

                            def more(n, unused, o=o, q=q, first=firsts[q], end=ends[q], low=bases[q]):
                                base = begin(low + (n + 1) * window)
                                at = pl.multiple_of(q * span + base, 16)
                                put(q, base, first, end, mixed(o, [at]))
                                return unused

                            lack = jnp.maximum(ends[q] - bases[q] - window, 0)
                            lax.fori_loop(0, (lack + window - 1) // window, more, 0)

                return unused

            lax.fori_loop(0, npatch // UNROLL, owners, 0)

        hot = (iota((span, span), 0) == pos_ref[...]).astype(F32).astype(BF)
        rows = y_ref[pl.ds(pl.multiple_of(step * span, span), span), :]
        turned = dot(lane_swap(width, local, levels), rows, NT).astype(BF)
        back = dot(turned, hot).astype(BF)
        out_ref[...] = jnp.where(mask_ref[...] == 1, back, land_ref[...])

    return pl.pallas_call(
        kernel,
        grid=(PARTS,),
        out_shape=jax.ShapeDtypeStruct((width, tiles), BF),
        in_specs=[SMEM, SMEM]
        + [pl.BlockSpec(memory_space=pl.ANY)] * count
        + [
            VMEM,
            pl.BlockSpec((1, span), lambda i: (0, i)),
            pl.BlockSpec((width, span), lambda i: (0, i)),
            pl.BlockSpec((1, span), lambda i: (0, i)),
        ],
        out_specs=pl.BlockSpec((width, span), lambda i: (0, i)),
        scratch_shapes=[
            pltpu.VMEM((slots, tiles, width), BF),
            pltpu.VMEM((npatch * local, slots * lanes), BF),
            pltpu.VMEM((tiles, width), BF),
            pltpu.SemaphoreType.DMA((count,)),
        ],
        compiler_params=params(60),
        name="mix_land",
    )(
        ids,
        starts,
        *flat,
        mixes.reshape(npatch * local, members),
        pos,
        land_rows,
        mask_row,
    )


def exact(a, b, dims=NN):
    return lax.dot_general(a, b, dims, precision=PRECISE, preferred_element_type=F32)


def screen_stats(ensemble, obs_value, obs_error):
    count, local, nobs = ensemble.shape
    members = count * local
    half = members // 2

    def kernel(in_ref, value_ref, error_ref, out_ref):
        rows = jnp.concatenate([in_ref[m].astype(F32) for m in range(count)], axis=0)
        center = jnp.mean(rows, axis=0, keepdims=True)
        inverse_sd = lax.rsqrt(error_ref[...])
        scaled = (rows - center) * inverse_sd
        innovation = (value_ref[...] - center) * inverse_sd
        gram = exact(scaled, scaled, NT)
        proj = exact(jnp.broadcast_to(innovation, (8, nobs)), scaled, NT)
        row, lane = iota((half, members), 0), iota((half, members), 1)
        top = gram[:half]
        from_low = jnp.logical_and(lane < half, lane >= row)
        out_ref[:half, :] = jnp.where(from_low, pltpu.roll(gram[half:], half, 1), top)
        diag = jnp.sum(jnp.where(row == lane, top, 0.0), axis=0, keepdims=True)
        tail = iota((8, members), 0)
        out_ref[half:, :] = jnp.where(tail == 0, diag, jnp.where(tail == 1, proj, 0.0))

    return pl.pallas_call(
        kernel,
        out_shape=jax.ShapeDtypeStruct((half + 8, members), F32),
        in_specs=[VMEM, VMEM, VMEM],
        out_specs=VMEM,
        compiler_params=params(16),
        name="screen_stats",
    )(ensemble, obs_value, obs_error)


def settle(own, near, listed, ids, offsets, local, npatch):
    members = own.shape[1]
    half = members // 2
    count = members // local
    names = listed.shape[1]

    def kernel(list_ref, id_ref, own_ref, *refs):
        near_refs = refs[: len(near)]
        cols_ref, out_ref, hold_ref = refs[len(near) :]
        total = own_ref[...]
        for d in range(len(near)):
            source = (id_ref[0] - offsets[d] + npatch) % npatch
            used = 0
            for i in range(names):
                used = used + jnp.where(list_ref[0, i] == source, 1, 0)
            total = total + used.astype(F32) * near_refs[d][...]
        packed = total[:half]
        row, lane = iota((half, members), 0), iota((half, members), 1)
        left = lane < half
        upper = jnp.logical_and(left, lane >= row)
        strict = jnp.logical_and(left, lane > row)
        top = jnp.where(upper, 0.0, packed)
        low = pltpu.roll(jnp.where(strict, packed, 0.0), half, 1)
        sides = jnp.concatenate([top, low], axis=0)
        on_diag = jnp.where(jnp.logical_and(left, lane == row), packed, 0.0)
        top_diag = jnp.where(row == lane, total[half : half + 1], 0.0)
        diag = jnp.concatenate([top_diag, pltpu.roll(on_diag, half, 1)], axis=0)
        eye = (iota((members, members), 0) == iota((members, members), 1)).astype(F32)
        system = sides + sides.T + diag + (members - 1.0) * eye
        scale = jnp.sum(jnp.sum(system * eye, axis=1, keepdims=True), axis=0, keepdims=True)
        upper_iter = system / scale
        middle = 1.5 * eye - 0.5 * upper_iter
        upper_iter = exact(upper_iter, middle)
        lower_iter = middle
        for step in range(SWEEPS - 1):
            middle = 1.5 * eye - 0.5 * exact(lower_iter, upper_iter)
            if step < SWEEPS - 2:
                upper_iter = exact(upper_iter, middle)
            lower_iter = exact(middle, lower_iter)
        inv_root = lower_iter * lax.rsqrt(scale)
        proj = jnp.broadcast_to(total[half + 1 : half + 2], (8, members))
        shift = exact(exact(proj, inv_root, NT), inv_root, NT)[:1]
        spread = shift + math.sqrt(members - 1.0) * inv_root
        hold_ref[...] = spread - jnp.mean(spread, axis=1, keepdims=True) + 1.0 / members
        mine = hold_ref[pl.ds(pl.multiple_of(id_ref[1] * local, local), local), :]
        cols_ref[...] = mine.astype(BF)
        flipped = mine.T
        blocks = jnp.concatenate(
            [flipped[m * local : (m + 1) * local] for m in range(count)], axis=1
        ).astype(BF)
        for p in range(npatch):
            out_ref[p] = blocks

    return pl.pallas_call(
        kernel,
        out_shape=(
            jax.ShapeDtypeStruct((local, members), BF),
            jax.ShapeDtypeStruct((npatch, local, members), BF),
        ),
        in_specs=[SMEM, SMEM] + [VMEM] * (1 + len(near)),
        out_specs=(VMEM, VMEM),
        scratch_shapes=[pltpu.VMEM((members, members), F32)],
        compiler_params=params(16),
        name="settle",
    )(listed, ids, own, *near)


def analysis(
    atmos,
    land,
    land_mask,
    tile_owner,
    tile_column,
    tile_weight,
    obs_value,
    observation_column,
    obs_error,
    loc_blocks,
):
    barrier = lax.optimization_barrier
    npatch = lax.axis_size("patch")
    mem_count = lax.axis_size("mem")
    local, levels, columns = atmos.shape
    layers, tiles = (land.shape[1], land.shape[2])
    bucket = 2 * tiles // npatch
    row_width = max(2, npatch // 8)
    mem_rank = lax.axis_index("mem")
    ids = jnp.stack([lax.axis_index("patch"), mem_rank]).astype(I32)

    atmos_rows = atmos.reshape(local * levels, columns)
    atmos_parts = [shifted(atmos_rows, "mem", s) for s in (1, -1, 2)]

    owners = tile_owner.reshape(1, tiles)
    land_rows = land.reshape(local * layers, tiles)
    mask_row = land_mask.reshape(1, tiles)
    ranks, pos, starts = order_tiles(owners, npatch)
    packed = bucket_tiles(
        land_rows,
        layers,
        tile_weight.reshape(tiles // 128, 128),
        land_mask.reshape(tiles // 128, 128),
        owners,
        ranks,
        tile_column.reshape(1, tiles),
        npatch,
        bucket,
    )
    received = lax.all_to_all(packed, "patch", split_axis=0, concat_axis=0, tiled=True)

    (first,) = sort_land(pos, land_rows, layers, 0, 1)
    first_prev = shifted(first, "mem", 1)
    first_next = shifted(first, "mem", -1)
    (second,) = sort_land(pos, land_rows, layers, 1, 1)
    second_prev = shifted(second, "mem", 1)
    second_next = shifted(second, "mem", -1)
    (rest,) = sort_land(pos, land_rows, layers, PARTS // 2, PARTS // 2)

    forecast = screen_forecast(
        received, atmos_rows, levels, observation_column.reshape(-1, 1), mem_count
    )
    forecast, first_prev, first_next, second_prev, second_next, rest = barrier(
        (forecast, first_prev, first_next, second_prev, second_next, rest)
    )
    ensemble = lax.all_to_all(forecast, "mem", split_axis=0, concat_axis=0, tiled=True)
    rest_prev = shifted(rest, "mem", 1)
    rest_next = shifted(rest, "mem", -1)
    first_far = shifted(first_prev, "mem", 1)
    second_far = shifted(second_prev, "mem", 1)

    own_stats = screen_stats(ensemble, obs_value.reshape(1, -1), obs_error.reshape(1, -1))
    offsets = (row_width, -row_width, 1, -1)
    near = [shifted(own_stats, "patch", o) for o in offsets]
    own_cols, mixes = settle(own_stats, near, loc_blocks, ids, offsets, local, npatch)
    own_cols, rest_next = barrier((own_cols, rest_next))
    rest_far = shifted(rest_next, "mem", -1)
    all_mixes = lax.all_to_all(mixes, "patch", split_axis=0, concat_axis=0, tiled=True)

    slot_source = [mem_rank, mem_rank - 1, mem_rank + 1, mem_rank - 2]
    atmos_out = 0.0
    for part, source in zip([atmos_rows] + atmos_parts, slot_source):
        rows = lax.dynamic_slice_in_dim(own_cols, (source % mem_count) * local, local, 1)
        atmos_out = atmos_out + jnp.einsum(
            "jk,klc->jlc", rows, part.reshape(local, levels, columns), preferred_element_type=F32
        )
    atmos_analysis = atmos_out.astype(BF)

    land_out = mix_land(
        [
            [first, second, rest],
            [first_prev, second_prev, rest_prev],
            [first_next, second_next, rest_next],
            [first_far, second_far, rest_far],
        ],
        ids,
        starts,
        all_mixes,
        pos,
        land_rows,
        mask_row,
        layers,
    )
    return (atmos_analysis, land_out.reshape(local, layers, tiles))


def solution(mesh):
    in_specs = (
        P("mem", None, "patch"),
        P("mem", None, "patch"),
        P("patch"),
        P("patch", None),
        P("patch"),
        P("patch"),
        P("patch"),
        P("patch"),
        P("patch"),
        P("patch", None),
    )
    out_specs = (P("mem", None, "patch"), P("mem", None, "patch"))
    return jax.shard_map(
        analysis, mesh=mesh, in_specs=in_specs, out_specs=out_specs, check_vma=False
    )
```

```python
import math

import jax
import jax.numpy as jnp
from jax import lax
from jax.experimental import pallas as pl
from jax.experimental.pallas import tpu as pltpu
from jax.sharding import PartitionSpec as P

SWEEPS = 10
PRECISE = lax.Precision.HIGHEST
BF = jnp.bfloat16
F32 = jnp.float32
I32 = jnp.int32

NN = (((1,), (0,)), ((), ()))
NT = (((1,), (1,)), ((), ()))


def dot(a, b, dims=NN):
    return lax.dot_general(a, b, dims, preferred_element_type=F32)


def iota(shape, axis):
    return lax.broadcasted_iota(I32, shape, axis)


VMEM = pl.BlockSpec(memory_space=pltpu.VMEM)
SMEM = pl.BlockSpec(memory_space=pltpu.SMEM)


def params(mib):
    return pltpu.CompilerParams(vmem_limit_bytes=mib * 1024 * 1024)


def shifted(value, axis, steps):
    count = lax.axis_size(axis)
    pairs = [(source, (source + steps) % count) for source in range(count)]
    return lax.ppermute(value, axis, pairs)


PARTS = 4
UNROLL = 4


def partner(patch, gap, npatch):
    return (patch + gap - 2 * gap * ((patch // abs(gap)) % 2) + npatch) % npatch


def swapped(value, gap, npatch):
    pairs = [(source, partner(source, gap, npatch)) for source in range(npatch)]
    return lax.ppermute(value, "patch", pairs)


def order_tiles(owners, npatch):
    tiles = owners.shape[1]
    block = 512
    per_part = tiles // PARTS // block

    def kernel(owner_ref, rank_ref, pos_ref, start_ref):
        before = (iota((block, block), 0) < iota((block, block), 1)).astype(BF)
        lower = (iota((npatch, npatch), 0) > iota((npatch, npatch), 1)).astype(BF)
        done = jnp.zeros((npatch, 1), F32)
        for part in range(PARTS):
            carry = jnp.zeros((npatch, 1), F32)
            held = []
            for c in range(per_part):
                at = (part * per_part + c) * block
                hot = owner_ref[:, at : at + block] == iota((npatch, block), 0)
                ahead = dot(hot.astype(BF), before) + carry
                hot = hot.astype(F32)
                carry = carry + jnp.sum(hot, axis=1, keepdims=True)
                held.append((at, hot, ahead))
            starts = dot(lower, jnp.broadcast_to(carry, (npatch, 128)).astype(BF))[:, :1]
            start_ref[:, part : part + 1] = starts.astype(I32)
            for at, hot, ahead in held:
                rank = jnp.sum(hot * (ahead + done), axis=0, keepdims=True)
                pos = jnp.sum(hot * (ahead + starts), axis=0, keepdims=True)
                rank_ref[:, at : at + block] = rank.astype(I32)
                pos_ref[:, at : at + block] = pos.astype(I32)
            done = done + carry
        start_ref[:, PARTS:] = jnp.zeros((npatch, PARTS), I32)

    return pl.pallas_call(
        kernel,
        out_shape=(
            jax.ShapeDtypeStruct((1, tiles), I32),
            jax.ShapeDtypeStruct((1, tiles), I32),
            jax.ShapeDtypeStruct((npatch, 2 * PARTS), I32),
        ),
        in_specs=[VMEM],
        out_specs=(VMEM, VMEM, VMEM),
        compiler_params=params(60),
        name="order_tiles",
    )(owners)


def bucket_tiles(land_rows, levels, weight, mask, owners, ranks, columns, npatch, bucket):
    width, tiles = land_rows.shape
    rows = width // levels
    low = 4
    high = npatch // low
    block = 1024
    steps = tiles // block

    def kernel(
        x_ref,
        weight_ref,
        mask_ref,
        owner_ref,
        rank_ref,
        col_ref,
        out_ref,
        acc_ref,
        cacc_ref,
        keep_ref,
    ):
        step = pl.program_id(0)
        owner = owner_ref[...]
        slot = (owner & (low - 1)) * bucket + rank_ref[...]
        hot = (iota((low * bucket, block), 0) == slot).astype(F32).astype(BF)
        group = owner >> 2
        surface = (iota((rows, width), 0) * levels == iota((rows, width), 1)).astype(F32)

        @pl.when(step == 0)
        def _():
            keep_ref[...] = weight_ref[...].astype(F32) * mask_ref[...].astype(F32)

        per_step = block // 128
        keep = keep_ref[pl.ds(pl.multiple_of(step * per_step, per_step), per_step), :]
        keep = jnp.concatenate([keep[c : c + 1] for c in range(per_step)], axis=1)
        value = (dot(surface.astype(BF), x_ref[...]) * keep).astype(BF)
        zero = jnp.zeros_like(value)
        picked = jnp.concatenate(
            [jnp.where(group == g, value, zero) for g in range(high)], axis=0
        )
        part = dot(picked, hot, NT)
        col = col_ref[...]
        half = iota((2 * high, block), 0)
        digit = jnp.where((half & 1) == 0, col >> 5, col & 31)
        digits = jnp.where((half >> 1) == group, digit, 0).astype(F32).astype(BF)
        cpart = dot(digits, hot, NT)

        @pl.when(step == 0)
        def _():
            acc_ref[...] = part
            cacc_ref[...] = cpart

        @pl.when(step > 0)
        def _():
            acc_ref[...] += part
            cacc_ref[...] += cpart

        @pl.when(step == steps - 1)
        def _():
            for o in range(npatch):
                g, b = o // low, o % low
                cut = slice(b * bucket, (b + 1) * bucket)
                out_ref[o, :rows, :] = acc_ref[g * rows : (g + 1) * rows, cut].astype(BF)
                out_ref[o, rows : rows + 2, :] = cacc_ref[2 * g : 2 * g + 2, cut].astype(BF)

    lane = pl.BlockSpec((1, block), lambda i: (0, i))
    return pl.pallas_call(
        kernel,
        grid=(steps,),
        out_shape=jax.ShapeDtypeStruct((npatch, rows + 2, bucket), BF),
        in_specs=[pl.BlockSpec((width, block), lambda i: (0, i)), VMEM, VMEM] + [lane] * 3,
        out_specs=pl.BlockSpec((npatch, rows + 2, bucket), lambda i: (0, 0, 0)),
        scratch_shapes=[
            pltpu.VMEM((high * rows, low * bucket), F32),
            pltpu.VMEM((2 * high, low * bucket), F32),
            pltpu.VMEM((tiles // 128, 128), F32),
        ],
        compiler_params=params(60),
        name="bucket_tiles",
    )(land_rows, weight, mask, owners, ranks, columns)


def lane_swap(rows, a, b):
    source = iota((rows, rows), 0)
    target = iota((rows, rows), 1)
    return ((source % b) * a + source // b == target).astype(F32).astype(BF)


def sort_land(pos, land_rows, levels, begin, end):
    width, tiles = land_rows.shape
    span = tiles // PARTS
    block = 512
    one = end - begin <= span and begin // span == (end - 1) // span
    taken = span if one else tiles
    shift = begin // span * span if one else 0

    def kernel(pos_ref, x_ref, out_ref):
        swap = lane_swap(width, width // levels, levels)
        for at in range(begin, end, block):
            part = at // span * span
            cut = slice(part - shift, part - shift + span)
            place = iota((block, span), 0) + (at - part)
            hot = (place == pos_ref[:, cut]).astype(F32).astype(BF)
            moved = dot(hot, x_ref[:, cut], NT).astype(BF)
            out_ref[at - begin : at - begin + block, :] = dot(moved, swap).astype(BF)

    return pl.pallas_call(
        kernel,
        grid=(1,),
        out_shape=jax.ShapeDtypeStruct((end - begin, width), BF),
        in_specs=[
            pl.BlockSpec((1, taken), lambda i: (0, shift // taken)),
            pl.BlockSpec((width, taken), lambda i: (0, shift // taken)),
        ],
        out_specs=pl.BlockSpec((end - begin, width), lambda i: (0, 0)),
        compiler_params=params(60),
        name="sort_land",
    )(pos, land_rows)


def screen_forecast(received, base_rows, levels, obs_column, copies):
    npatch, rows2, _ = received.shape
    rows = rows2 - 2
    nobs = obs_column.shape[0]
    width, columns = base_rows.shape
    group = 8

    def kernel(in_ref, base_ref, obs_ref, out_ref):
        obs = obs_ref[...]
        place = iota((nobs, columns), 1)
        surface = (iota((rows, width), 0) * levels == iota((rows, width), 1)).astype(F32)
        base = dot(surface.astype(BF), base_ref[...]).astype(BF)
        acc = dot(base, (obs == place).astype(F32).astype(BF), NT)
        for g in range(npatch // group):
            values = jnp.concatenate(
                [in_ref[g * group + i, :rows, :] for i in range(group)], axis=1
            )
            digits = jnp.concatenate(
                [in_ref[g * group + i, rows:, :] for i in range(group)], axis=1
            ).astype(F32)
            col = (digits[0:1] * 32.0 + digits[1:2]).astype(I32)
            acc = acc + dot(values, (obs == col).astype(F32).astype(BF), NT)
        value = acc.astype(BF)
        for m in range(copies):
            out_ref[m] = value

    return pl.pallas_call(
        kernel,
        out_shape=jax.ShapeDtypeStruct((copies, rows, nobs), BF),
        in_specs=[VMEM, VMEM, VMEM],
        out_specs=VMEM,
        compiler_params=params(24),
        name="screen_forecast",
    )(received, base_rows, obs_column)


def mix_land(pieces, ids, starts, mixes, pos, land_rows, mask_row, levels):
    slots = len(pieces)
    flat = [piece for group in pieces for piece in group]
    places = [
        (s, sum(p.shape[0] for p in group[:i]))
        for s, group in enumerate(pieces)
        for i in range(len(group))
    ]
    width, tiles = land_rows.shape
    local = width // levels
    npatch = mixes.shape[0]
    members = mixes.shape[2]
    span = tiles // PARTS
    window = 48
    lanes = 128
    count = len(flat)

    def kernel(id_ref, start_ref, *refs):
        piece_refs = refs[:count]
        mix_ref, pos_ref, land_ref, mask_ref, out_ref = refs[count : count + 5]
        state_ref, tiled_ref, y_ref, sems = refs[count + 5 :]
        step = pl.program_id(0)

        @pl.when(step == 0)
        def _():
            copies = [
                pltpu.make_async_copy(
                    piece_refs[i],
                    state_ref.at[s, pl.ds(at, piece_refs[i].shape[0]), :],
                    sems.at[i],
                )
                for i, (s, at) in enumerate(places)
            ]
            for copy in copies:
                copy.start()
            for s in range(slots):
                spread = (
                    iota((members, lanes), 0)
                    == (iota((members, lanes), 1) & (local - 1)) + (id_ref[1] + (0, slots - 1, 1, 2)[s]) % slots * local
                )
                tiled_ref[:, s * lanes : (s + 1) * lanes] = dot(
                    mix_ref[...], spread.astype(F32).astype(BF)
                ).astype(BF)
            lane_level = iota((local, lanes), 1) // local
            for copy in copies:
                copy.wait()

            def weight_of(o, s):
                at = pl.multiple_of(o * local, local)
                parts = []
                for t in (s, s + 1):
                    small = tiled_ref[pl.ds(at, local), t * lanes : (t + 1) * lanes]
                    zero = jnp.zeros_like(small)
                    parts += [
                        jnp.where(lane_level == l, small, zero) for l in range(lanes // local)
                    ]
                return jnp.concatenate(parts, axis=0)

            def mixed(o, cuts):
                acc = None
                for s in range(0, slots, 2):
                    rows = [
                        jnp.concatenate(
                            [
                                state_ref[t, pl.ds(at, window), h * lanes : (h + 1) * lanes]
                                for t in (s, s + 1)
                            ],
                            axis=1,
                        )
                        for h in range(width // lanes)
                        for at in cuts
                    ]
                    part = dot(jnp.concatenate(rows, axis=0), weight_of(o, s))
                    acc = part if acc is None else acc + part
                half = len(cuts) * window
                return jnp.concatenate(
                    [acc[h * half : (h + 1) * half] for h in range(width // lanes)], axis=1
                ).astype(BF)

            def put(part, base, first, end, value):
                at = pl.multiple_of(part * span + base, 16)
                row = iota((window, width), 0) + base
                keep = row >= first
                if end is not None:
                    keep = jnp.logical_and(keep, row < end)
                old = y_ref[pl.ds(at, window), :]
                y_ref[pl.ds(at, window), :] = jnp.where(keep, value, old)

            def begin(first):
                return pl.multiple_of(jnp.minimum((first // 16) * 16, span - window), 16)

            def bounds(o):
                firsts = [start_ref[o, q] for q in range(PARTS)]
                after = jnp.minimum(o + 1, npatch - 1)
                ends = [
                    jnp.where(o == npatch - 1, span, start_ref[after, q]) for q in range(PARTS)
                ]
                return firsts, ends, [begin(first) for first in firsts]

            def owners(i, unused):
                group = [i * UNROLL + u for u in range(UNROLL)]
                limits = [bounds(o) for o in group]
                values = [
                    mixed(o, [pl.multiple_of(q * span + bases[q], 16) for q in range(PARTS)])
                    for o, (firsts, ends, bases) in zip(group, limits)
                ]
                for value, (firsts, ends, bases) in zip(values, limits):
                    for q in range(PARTS):
                        put(q, bases[q], firsts[q], None, value[q * window : (q + 1) * window])
                most = 0
                for firsts, ends, bases in limits:
                    for q in range(PARTS):
                        most = jnp.maximum(most, ends[q] - bases[q] - window)

                @pl.when(most > 0)
                def _():
                    for o, (firsts, ends, bases) in zip(group, limits):
                        for q in range(PARTS):

                            def more(n, unused, o=o, q=q, first=firsts[q], end=ends[q], low=bases[q]):
                                base = begin(low + (n + 1) * window)
                                at = pl.multiple_of(q * span + base, 16)
                                put(q, base, first, end, mixed(o, [at]))
                                return unused

                            lack = jnp.maximum(ends[q] - bases[q] - window, 0)
                            lax.fori_loop(0, (lack + window - 1) // window, more, 0)

                return unused

            lax.fori_loop(0, npatch // UNROLL, owners, 0)

        hot = (iota((span, span), 0) == pos_ref[...]).astype(F32).astype(BF)
        rows = y_ref[pl.ds(pl.multiple_of(step * span, span), span), :]
        turned = dot(lane_swap(width, local, levels), rows, NT).astype(BF)
        back = dot(turned, hot).astype(BF)
        out_ref[...] = jnp.where(mask_ref[...] == 1, back, land_ref[...])

    return pl.pallas_call(
        kernel,
        grid=(PARTS,),
        out_shape=jax.ShapeDtypeStruct((width, tiles), BF),
        in_specs=[SMEM, SMEM]
        + [pl.BlockSpec(memory_space=pl.ANY)] * count
        + [
            VMEM,
            pl.BlockSpec((1, span), lambda i: (0, i)),
            pl.BlockSpec((width, span), lambda i: (0, i)),
            pl.BlockSpec((1, span), lambda i: (0, i)),
        ],
        out_specs=pl.BlockSpec((width, span), lambda i: (0, i)),
        scratch_shapes=[
            pltpu.VMEM((slots, tiles, width), BF),
            pltpu.VMEM((npatch * local, slots * lanes), BF),
            pltpu.VMEM((tiles, width), BF),
            pltpu.SemaphoreType.DMA((count,)),
        ],
        compiler_params=params(60),
        name="mix_land",
    )(
        ids,
        starts,
        *flat,
        mixes.reshape(npatch * local, members),
        pos,
        land_rows,
        mask_row,
    )


def exact(a, b, dims=NN):
    return lax.dot_general(a, b, dims, precision=PRECISE, preferred_element_type=F32)


def screen_stats(ensemble, obs_value, obs_error):
    count, local, nobs = ensemble.shape
    members = count * local
    half = members // 2

    def kernel(in_ref, value_ref, error_ref, out_ref):
        rows = jnp.concatenate([in_ref[m].astype(F32) for m in range(count)], axis=0)
        center = jnp.mean(rows, axis=0, keepdims=True)
        inverse_sd = lax.rsqrt(error_ref[...])
        scaled = (rows - center) * inverse_sd
        innovation = (value_ref[...] - center) * inverse_sd
        gram = exact(scaled, scaled, NT)
        proj = exact(jnp.broadcast_to(innovation, (8, nobs)), scaled, NT)
        row, lane = iota((half, members), 0), iota((half, members), 1)
        top = gram[:half]
        from_low = jnp.logical_and(lane < half, lane >= row)
        out_ref[:half, :] = jnp.where(from_low, pltpu.roll(gram[half:], half, 1), top)
        diag = jnp.sum(jnp.where(row == lane, top, 0.0), axis=0, keepdims=True)
        tail = iota((8, members), 0)
        out_ref[half:, :] = jnp.where(tail == 0, diag, jnp.where(tail == 1, proj, 0.0))

    return pl.pallas_call(
        kernel,
        out_shape=jax.ShapeDtypeStruct((half + 8, members), F32),
        in_specs=[VMEM, VMEM, VMEM],
        out_specs=VMEM,
        compiler_params=params(16),
        name="screen_stats",
    )(ensemble, obs_value, obs_error)


def settle(own, near, listed, ids, gaps, local, npatch):
    members = own.shape[1]
    half = members // 2
    count = members // local
    names = listed.shape[1]

    def kernel(list_ref, id_ref, own_ref, *refs):
        near_refs = refs[: len(near)]
        cols_ref, out_ref, hold_ref = refs[len(near) :]
        total = own_ref[...]
        for d in range(len(near)):
            source = partner(id_ref[0], gaps[d], npatch)
            used = 0
            for i in range(names):
                used = used + jnp.where(list_ref[0, i] == source, 1, 0)
            total = total + used.astype(F32) * near_refs[d][...]
        packed = total[:half]
        row, lane = iota((half, members), 0), iota((half, members), 1)
        left = lane < half
        upper = jnp.logical_and(left, lane >= row)
        strict = jnp.logical_and(left, lane > row)
        top = jnp.where(upper, 0.0, packed)
        low = pltpu.roll(jnp.where(strict, packed, 0.0), half, 1)
        sides = jnp.concatenate([top, low], axis=0)
        on_diag = jnp.where(jnp.logical_and(left, lane == row), packed, 0.0)
        top_diag = jnp.where(row == lane, total[half : half + 1], 0.0)
        diag = jnp.concatenate([top_diag, pltpu.roll(on_diag, half, 1)], axis=0)
        eye = (iota((members, members), 0) == iota((members, members), 1)).astype(F32)
        system = sides + sides.T + diag + (members - 1.0) * eye
        scale = jnp.sum(jnp.sum(system * eye, axis=1, keepdims=True), axis=0, keepdims=True)
        upper_iter = system / scale
        middle = 1.5 * eye - 0.5 * upper_iter
        upper_iter = exact(upper_iter, middle)
        lower_iter = middle
        for step in range(SWEEPS - 1):
            middle = 1.5 * eye - 0.5 * exact(lower_iter, upper_iter)
            if step < SWEEPS - 2:
                upper_iter = exact(upper_iter, middle)
            lower_iter = exact(middle, lower_iter)
        inv_root = lower_iter * lax.rsqrt(scale)
        proj = jnp.broadcast_to(total[half + 1 : half + 2], (8, members))
        shift = exact(exact(proj, inv_root, NT), inv_root, NT)[:1]
        spread = shift + math.sqrt(members - 1.0) * inv_root
        hold_ref[...] = spread - jnp.mean(spread, axis=1, keepdims=True) + 1.0 / members
        mine = hold_ref[pl.ds(pl.multiple_of(id_ref[1] * local, local), local), :]
        cols_ref[...] = mine.astype(BF)
        flipped = mine.T
        blocks = jnp.concatenate(
            [flipped[m * local : (m + 1) * local] for m in range(count)], axis=1
        ).astype(BF)
        for p in range(npatch):
            out_ref[p] = blocks

    return pl.pallas_call(
        kernel,
        out_shape=(
            jax.ShapeDtypeStruct((local, members), BF),
            jax.ShapeDtypeStruct((npatch, local, members), BF),
        ),
        in_specs=[SMEM, SMEM] + [VMEM] * (1 + len(near)),
        out_specs=(VMEM, VMEM),
        scratch_shapes=[pltpu.VMEM((members, members), F32)],
        compiler_params=params(16),
        name="settle",
    )(listed, ids, own, *near)


def analysis(
    atmos,
    land,
    land_mask,
    tile_owner,
    tile_column,
    tile_weight,
    obs_value,
    observation_column,
    obs_error,
    loc_blocks,
):
    barrier = lax.optimization_barrier
    npatch = lax.axis_size("patch")
    mem_count = lax.axis_size("mem")
    local, levels, columns = atmos.shape
    layers, tiles = (land.shape[1], land.shape[2])
    bucket = 2 * tiles // npatch
    row_width = max(2, npatch // 8)
    mem_rank = lax.axis_index("mem")
    ids = jnp.stack([lax.axis_index("patch"), mem_rank]).astype(I32)

    atmos_rows = atmos.reshape(local * levels, columns)
    atmos_parts = [shifted(atmos_rows, "mem", s) for s in (1, -1, 2)]

    owners = tile_owner.reshape(1, tiles)
    land_rows = land.reshape(local * layers, tiles)
    mask_row = land_mask.reshape(1, tiles)
    ranks, pos, starts = order_tiles(owners, npatch)
    packed = bucket_tiles(
        land_rows,
        layers,
        tile_weight.reshape(tiles // 128, 128),
        land_mask.reshape(tiles // 128, 128),
        owners,
        ranks,
        tile_column.reshape(1, tiles),
        npatch,
        bucket,
    )
    received = lax.all_to_all(packed, "patch", split_axis=0, concat_axis=0, tiled=True)

    early = (tiles // PARTS, 3 * tiles // (2 * PARTS))
    first = sort_land(pos, land_rows, layers, 0, early[0])
    first_prev = shifted(first, "mem", 1)
    first_next = shifted(first, "mem", -1)
    second = sort_land(pos, land_rows, layers, *early)
    second_prev = shifted(second, "mem", 1)
    second_next = shifted(second, "mem", -1)
    rest = sort_land(pos, land_rows, layers, early[1], tiles)

    forecast = screen_forecast(
        received, atmos_rows, levels, observation_column.reshape(-1, 1), mem_count
    )
    forecast, first_prev, first_next, second_prev, second_next, rest = barrier(
        (forecast, first_prev, first_next, second_prev, second_next, rest)
    )
    ensemble = lax.all_to_all(forecast, "mem", split_axis=0, concat_axis=0, tiled=True)
    rest_prev = shifted(rest, "mem", 1)
    rest_next = shifted(rest, "mem", -1)
    first_far = shifted(first_prev, "mem", 1)
    second_far = shifted(second_prev, "mem", 1)

    own_stats = screen_stats(ensemble, obs_value.reshape(1, -1), obs_error.reshape(1, -1))
    gaps = (1, -1, row_width, -row_width)
    near = [swapped(own_stats, gap, npatch) for gap in gaps]
    own_cols, mixes = settle(own_stats, near, loc_blocks, ids, gaps, local, npatch)
    own_cols, rest_next = barrier((own_cols, rest_next))
    rest_far = shifted(rest_next, "mem", -1)
    all_mixes = lax.all_to_all(mixes, "patch", split_axis=0, concat_axis=0, tiled=True)

    slot_source = [mem_rank, mem_rank - 1, mem_rank + 1, mem_rank - 2]
    atmos_out = 0.0
    for part, source in zip([atmos_rows] + atmos_parts, slot_source):
        rows = lax.dynamic_slice_in_dim(own_cols, (source % mem_count) * local, local, 1)
        atmos_out = atmos_out + jnp.einsum(
            "jk,klc->jlc", rows, part.reshape(local, levels, columns), preferred_element_type=F32
        )
    atmos_analysis = atmos_out.astype(BF)

    land_out = mix_land(
        [
            [first, second, rest],
            [first_prev, second_prev, rest_prev],
            [first_next, second_next, rest_next],
            [first_far, second_far, rest_far],
        ],
        ids,
        starts,
        all_mixes,
        pos,
        land_rows,
        mask_row,
        layers,
    )
    return (atmos_analysis, land_out.reshape(local, layers, tiles))


def solution(mesh):
    in_specs = (
        P("mem", None, "patch"),
        P("mem", None, "patch"),
        P("patch"),
        P("patch", None),
        P("patch"),
        P("patch"),
        P("patch"),
        P("patch"),
        P("patch"),
        P("patch", None),
    )
    out_specs = (P("mem", None, "patch"), P("mem", None, "patch"))
    return jax.shard_map(
        analysis, mesh=mesh, in_specs=in_specs, out_specs=out_specs, check_vma=False
    )
```

```python
import math

import jax
import jax.numpy as jnp
from jax import lax
from jax.experimental import pallas as pl
from jax.experimental.pallas import tpu as pltpu
from jax.sharding import PartitionSpec as P

SWEEPS = 10
PRECISE = lax.Precision.HIGHEST
BF = jnp.bfloat16
F32 = jnp.float32
I32 = jnp.int32

NN = (((1,), (0,)), ((), ()))
NT = (((1,), (1,)), ((), ()))


def dot(a, b, dims=NN):
    return lax.dot_general(a, b, dims, preferred_element_type=F32)


def iota(shape, axis):
    return lax.broadcasted_iota(I32, shape, axis)


VMEM = pl.BlockSpec(memory_space=pltpu.VMEM)
SMEM = pl.BlockSpec(memory_space=pltpu.SMEM)


def params(mib):
    return pltpu.CompilerParams(vmem_limit_bytes=mib * 1024 * 1024)


def shifted(value, axis, steps):
    count = lax.axis_size(axis)
    pairs = [(source, (source + steps) % count) for source in range(count)]
    return lax.ppermute(value, axis, pairs)


PARTS = 4
UNROLL = 4


def partner(patch, gap, npatch):
    return (patch + gap - 2 * gap * ((patch // abs(gap)) % 2) + npatch) % npatch


def swapped(value, gap, npatch):
    pairs = [(source, partner(source, gap, npatch)) for source in range(npatch)]
    return lax.ppermute(value, "patch", pairs)


def order_tiles(owners, npatch):
    tiles = owners.shape[1]
    block = 512
    per_part = tiles // PARTS // block

    def kernel(owner_ref, rank_ref, pos_ref, start_ref):
        before = (iota((block, block), 0) < iota((block, block), 1)).astype(BF)
        lower = (iota((npatch, npatch), 0) > iota((npatch, npatch), 1)).astype(BF)
        done = jnp.zeros((npatch, 1), F32)
        for part in range(PARTS):
            carry = jnp.zeros((npatch, 1), F32)
            held = []
            for c in range(per_part):
                at = (part * per_part + c) * block
                hot = owner_ref[:, at : at + block] == iota((npatch, block), 0)
                ahead = dot(hot.astype(BF), before) + carry
                hot = hot.astype(F32)
                carry = carry + jnp.sum(hot, axis=1, keepdims=True)
                held.append((at, hot, ahead))
            starts = dot(lower, jnp.broadcast_to(carry, (npatch, 128)).astype(BF))[:, :1]
            start_ref[:, part : part + 1] = starts.astype(I32)
            for at, hot, ahead in held:
                rank = jnp.sum(hot * (ahead + done), axis=0, keepdims=True)
                pos = jnp.sum(hot * (ahead + starts), axis=0, keepdims=True)
                rank_ref[:, at : at + block] = rank.astype(I32)
                pos_ref[:, at : at + block] = pos.astype(I32)
            done = done + carry
        start_ref[:, PARTS:] = jnp.zeros((npatch, PARTS), I32)

    return pl.pallas_call(
        kernel,
        out_shape=(
            jax.ShapeDtypeStruct((1, tiles), I32),
            jax.ShapeDtypeStruct((1, tiles), I32),
            jax.ShapeDtypeStruct((npatch, 2 * PARTS), I32),
        ),
        in_specs=[VMEM],
        out_specs=(VMEM, VMEM, VMEM),
        compiler_params=params(60),
        name="order_tiles",
    )(owners)


def bucket_tiles(land_rows, levels, weight, mask, owners, ranks, columns, npatch, bucket):
    width, tiles = land_rows.shape
    rows = width // levels
    low = 4
    high = npatch // low
    block = 1024
    steps = tiles // block

    def kernel(
        x_ref,
        weight_ref,
        mask_ref,
        owner_ref,
        rank_ref,
        col_ref,
        out_ref,
        acc_ref,
        cacc_ref,
        keep_ref,
    ):
        step = pl.program_id(0)
        owner = owner_ref[...]
        slot = (owner & (low - 1)) * bucket + rank_ref[...]
        hot = (iota((low * bucket, block), 0) == slot).astype(F32).astype(BF)
        group = owner >> 2
        surface = (iota((rows, width), 0) * levels == iota((rows, width), 1)).astype(F32)

        @pl.when(step == 0)
        def _():
            keep_ref[...] = weight_ref[...].astype(F32) * mask_ref[...].astype(F32)

        per_step = block // 128
        keep = keep_ref[pl.ds(pl.multiple_of(step * per_step, per_step), per_step), :]
        keep = jnp.concatenate([keep[c : c + 1] for c in range(per_step)], axis=1)
        value = (dot(surface.astype(BF), x_ref[...]) * keep).astype(BF)
        zero = jnp.zeros_like(value)
        picked = jnp.concatenate(
            [jnp.where(group == g, value, zero) for g in range(high)], axis=0
        )
        part = dot(picked, hot, NT)
        col = col_ref[...]
        half = iota((2 * high, block), 0)
        digit = jnp.where((half & 1) == 0, col >> 5, col & 31)
        digits = jnp.where((half >> 1) == group, digit, 0).astype(F32).astype(BF)
        cpart = dot(digits, hot, NT)

        @pl.when(step == 0)
        def _():
            acc_ref[...] = part
            cacc_ref[...] = cpart

        @pl.when(step > 0)
        def _():
            acc_ref[...] += part
            cacc_ref[...] += cpart

        @pl.when(step == steps - 1)
        def _():
            for o in range(npatch):
                g, b = o // low, o % low
                cut = slice(b * bucket, (b + 1) * bucket)
                out_ref[o, :rows, :] = acc_ref[g * rows : (g + 1) * rows, cut].astype(BF)
                out_ref[o, rows : rows + 2, :] = cacc_ref[2 * g : 2 * g + 2, cut].astype(BF)

    lane = pl.BlockSpec((1, block), lambda i: (0, i))
    return pl.pallas_call(
        kernel,
        grid=(steps,),
        out_shape=jax.ShapeDtypeStruct((npatch, rows + 2, bucket), BF),
        in_specs=[pl.BlockSpec((width, block), lambda i: (0, i)), VMEM, VMEM] + [lane] * 3,
        out_specs=pl.BlockSpec((npatch, rows + 2, bucket), lambda i: (0, 0, 0)),
        scratch_shapes=[
            pltpu.VMEM((high * rows, low * bucket), F32),
            pltpu.VMEM((2 * high, low * bucket), F32),
            pltpu.VMEM((tiles // 128, 128), F32),
        ],
        compiler_params=params(60),
        name="bucket_tiles",
    )(land_rows, weight, mask, owners, ranks, columns)


def lane_swap(rows, a, b):
    source = iota((rows, rows), 0)
    target = iota((rows, rows), 1)
    return ((source % b) * a + source // b == target).astype(F32).astype(BF)


def sort_land(pos, land_rows, levels, begin, end):
    width, tiles = land_rows.shape
    span = tiles // PARTS
    block = 512
    one = end - begin <= span and begin // span == (end - 1) // span
    taken = span if one else tiles
    shift = begin // span * span if one else 0

    def kernel(pos_ref, x_ref, out_ref):
        swap = lane_swap(width, width // levels, levels)
        for at in range(begin, end, block):
            part = at // span * span
            cut = slice(part - shift, part - shift + span)
            place = iota((block, span), 0) + (at - part)
            hot = (place == pos_ref[:, cut]).astype(F32).astype(BF)
            moved = dot(hot, x_ref[:, cut], NT).astype(BF)
            out_ref[at - begin : at - begin + block, :] = dot(moved, swap).astype(BF)

    return pl.pallas_call(
        kernel,
        grid=(1,),
        out_shape=jax.ShapeDtypeStruct((end - begin, width), BF),
        in_specs=[
            pl.BlockSpec((1, taken), lambda i: (0, shift // taken)),
            pl.BlockSpec((width, taken), lambda i: (0, shift // taken)),
        ],
        out_specs=pl.BlockSpec((end - begin, width), lambda i: (0, 0)),
        compiler_params=params(60),
        name="sort_land",
    )(pos, land_rows)


def screen_forecast(received, base_rows, levels, obs_column, copies):
    npatch, rows2, _ = received.shape
    rows = rows2 - 2
    nobs = obs_column.shape[0]
    width, columns = base_rows.shape
    group = 8

    def kernel(in_ref, base_ref, obs_ref, out_ref):
        obs = obs_ref[...]
        place = iota((nobs, columns), 1)
        surface = (iota((rows, width), 0) * levels == iota((rows, width), 1)).astype(F32)
        base = dot(surface.astype(BF), base_ref[...]).astype(BF)
        acc = dot(base, (obs == place).astype(F32).astype(BF), NT)
        for g in range(npatch // group):
            values = jnp.concatenate(
                [in_ref[g * group + i, :rows, :] for i in range(group)], axis=1
            )
            digits = jnp.concatenate(
                [in_ref[g * group + i, rows:, :] for i in range(group)], axis=1
            ).astype(F32)
            col = (digits[0:1] * 32.0 + digits[1:2]).astype(I32)
            acc = acc + dot(values, (obs == col).astype(F32).astype(BF), NT)
        value = acc.astype(BF)
        for m in range(copies):
            out_ref[m] = value

    return pl.pallas_call(
        kernel,
        out_shape=jax.ShapeDtypeStruct((copies, rows, nobs), BF),
        in_specs=[VMEM, VMEM, VMEM],
        out_specs=VMEM,
        compiler_params=params(24),
        name="screen_forecast",
    )(received, base_rows, obs_column)


def mix_land(pieces, ids, starts, mixes, pos, land_rows, mask_row, levels):
    slots = len(pieces)
    flat = [piece for group in pieces for piece in group]
    places = [
        (s, sum(p.shape[0] for p in group[:i]))
        for s, group in enumerate(pieces)
        for i in range(len(group))
    ]
    width, tiles = land_rows.shape
    local = width // levels
    npatch = mixes.shape[0]
    members = mixes.shape[2]
    span = tiles // PARTS
    window = 48
    lanes = 128
    count = len(flat)

    def kernel(id_ref, start_ref, *refs):
        piece_refs = refs[:count]
        mix_ref, pos_ref, land_ref, mask_ref, out_ref = refs[count : count + 5]
        state_ref, tiled_ref, y_ref, sems = refs[count + 5 :]
        step = pl.program_id(0)

        @pl.when(step == 0)
        def _():
            copies = [
                pltpu.make_async_copy(
                    piece_refs[i],
                    state_ref.at[s, pl.ds(at, piece_refs[i].shape[0]), :],
                    sems.at[i],
                )
                for i, (s, at) in enumerate(places)
            ]
            for copy in copies:
                copy.start()
            for s in range(slots):
                spread = (
                    iota((members, lanes), 0)
                    == (iota((members, lanes), 1) & (local - 1)) + (id_ref[1] + (0, slots - 1, 1, 2)[s]) % slots * local
                )
                tiled_ref[:, s * lanes : (s + 1) * lanes] = dot(
                    mix_ref[...], spread.astype(F32).astype(BF)
                ).astype(BF)
            lane_level = iota((local, lanes), 1) // local
            for copy in copies:
                copy.wait()

            def weight_of(o, s):
                at = pl.multiple_of(o * local, local)
                parts = []
                for t in (s, s + 1):
                    small = tiled_ref[pl.ds(at, local), t * lanes : (t + 1) * lanes]
                    zero = jnp.zeros_like(small)
                    parts += [
                        jnp.where(lane_level == l, small, zero) for l in range(lanes // local)
                    ]
                return jnp.concatenate(parts, axis=0)

            def mixed(o, cuts):
                acc = None
                for s in range(0, slots, 2):
                    rows = [
                        jnp.concatenate(
                            [
                                state_ref[t, pl.ds(at, window), h * lanes : (h + 1) * lanes]
                                for t in (s, s + 1)
                            ],
                            axis=1,
                        )
                        for h in range(width // lanes)
                        for at in cuts
                    ]
                    part = dot(jnp.concatenate(rows, axis=0), weight_of(o, s))
                    acc = part if acc is None else acc + part
                half = len(cuts) * window
                return jnp.concatenate(
                    [acc[h * half : (h + 1) * half] for h in range(width // lanes)], axis=1
                ).astype(BF)

            def put(part, base, first, end, value):
                at = pl.multiple_of(part * span + base, 16)
                row = iota((window, width), 0) + base
                keep = row >= first
                if end is not None:
                    keep = jnp.logical_and(keep, row < end)
                old = y_ref[pl.ds(at, window), :]
                y_ref[pl.ds(at, window), :] = jnp.where(keep, value, old)

            def begin(first):
                return pl.multiple_of(jnp.minimum((first // 16) * 16, span - window), 16)

            def bounds(o):
                firsts = [start_ref[o, q] for q in range(PARTS)]
                after = jnp.minimum(o + 1, npatch - 1)
                ends = [
                    jnp.where(o == npatch - 1, span, start_ref[after, q]) for q in range(PARTS)
                ]
                return firsts, ends, [begin(first) for first in firsts]

            def owners(i, unused):
                group = [i * UNROLL + u for u in range(UNROLL)]
                limits = [bounds(o) for o in group]
                values = [
                    mixed(o, [pl.multiple_of(q * span + bases[q], 16) for q in range(PARTS)])
                    for o, (firsts, ends, bases) in zip(group, limits)
                ]
                for value, (firsts, ends, bases) in zip(values, limits):
                    for q in range(PARTS):
                        put(q, bases[q], firsts[q], None, value[q * window : (q + 1) * window])
                most = 0
                for firsts, ends, bases in limits:
                    for q in range(PARTS):
                        most = jnp.maximum(most, ends[q] - bases[q] - window)

                @pl.when(most > 0)
                def _():
                    for o, (firsts, ends, bases) in zip(group, limits):
                        lacks = [
                            jnp.maximum(ends[q] - bases[q] - window, 0) for q in range(PARTS)
                        ]

                        @pl.when(lacks[0] + lacks[1] + lacks[2] + lacks[3] > 0)
                        def _():
                            for q in range(PARTS):

                                def more(n, unused, q=q):
                                    base = begin(bases[q] + (n + 1) * window)
                                    at = pl.multiple_of(q * span + base, 16)
                                    put(q, base, firsts[q], ends[q], mixed(o, [at]))
                                    return unused

                                lax.fori_loop(0, (lacks[q] + window - 1) // window, more, 0)

                return unused

            lax.fori_loop(0, npatch // UNROLL, owners, 0)

        hot = (iota((span, span), 0) == pos_ref[...]).astype(F32).astype(BF)
        rows = y_ref[pl.ds(pl.multiple_of(step * span, span), span), :]
        turned = dot(lane_swap(width, local, levels), rows, NT).astype(BF)
        back = dot(turned, hot).astype(BF)
        out_ref[...] = jnp.where(mask_ref[...] == 1, back, land_ref[...])

    return pl.pallas_call(
        kernel,
        grid=(PARTS,),
        out_shape=jax.ShapeDtypeStruct((width, tiles), BF),
        in_specs=[SMEM, SMEM]
        + [pl.BlockSpec(memory_space=pl.ANY)] * count
        + [
            VMEM,
            pl.BlockSpec((1, span), lambda i: (0, i)),
            pl.BlockSpec((width, span), lambda i: (0, i)),
            pl.BlockSpec((1, span), lambda i: (0, i)),
        ],
        out_specs=pl.BlockSpec((width, span), lambda i: (0, i)),
        scratch_shapes=[
            pltpu.VMEM((slots, tiles, width), BF),
            pltpu.VMEM((npatch * local, slots * lanes), BF),
            pltpu.VMEM((tiles, width), BF),
            pltpu.SemaphoreType.DMA((count,)),
        ],
        compiler_params=params(60),
        name="mix_land",
    )(
        ids,
        starts,
        *flat,
        mixes.reshape(npatch * local, members),
        pos,
        land_rows,
        mask_row,
    )


def exact(a, b, dims=NN):
    return lax.dot_general(a, b, dims, precision=PRECISE, preferred_element_type=F32)


def screen_stats(ensemble, obs_value, obs_error):
    count, local, nobs = ensemble.shape
    members = count * local
    half = members // 2

    def kernel(in_ref, value_ref, error_ref, out_ref):
        rows = jnp.concatenate([in_ref[m].astype(F32) for m in range(count)], axis=0)
        center = jnp.mean(rows, axis=0, keepdims=True)
        inverse_sd = lax.rsqrt(error_ref[...])
        scaled = (rows - center) * inverse_sd
        innovation = (value_ref[...] - center) * inverse_sd
        gram = exact(scaled, scaled, NT)
        proj = exact(jnp.broadcast_to(innovation, (8, nobs)), scaled, NT)
        row, lane = iota((half, members), 0), iota((half, members), 1)
        top = gram[:half]
        from_low = jnp.logical_and(lane < half, lane >= row)
        out_ref[:half, :] = jnp.where(from_low, pltpu.roll(gram[half:], half, 1), top)
        diag = jnp.sum(jnp.where(row == lane, top, 0.0), axis=0, keepdims=True)
        tail = iota((8, members), 0)
        out_ref[half:, :] = jnp.where(tail == 0, diag, jnp.where(tail == 1, proj, 0.0))

    return pl.pallas_call(
        kernel,
        out_shape=jax.ShapeDtypeStruct((half + 8, members), F32),
        in_specs=[VMEM, VMEM, VMEM],
        out_specs=VMEM,
        compiler_params=params(16),
        name="screen_stats",
    )(ensemble, obs_value, obs_error)


def settle(own, near, listed, ids, gaps, local, npatch):
    members = own.shape[1]
    half = members // 2
    count = members // local
    names = listed.shape[1]

    def kernel(list_ref, id_ref, own_ref, *refs):
        near_refs = refs[: len(near)]
        cols_ref, out_ref, hold_ref = refs[len(near) :]
        total = own_ref[...]
        for d in range(len(near)):
            source = partner(id_ref[0], gaps[d], npatch)
            used = 0
            for i in range(names):
                used = used + jnp.where(list_ref[0, i] == source, 1, 0)
            total = total + used.astype(F32) * near_refs[d][...]
        packed = total[:half]
        row, lane = iota((half, members), 0), iota((half, members), 1)
        left = lane < half
        upper = jnp.logical_and(left, lane >= row)
        strict = jnp.logical_and(left, lane > row)
        top = jnp.where(upper, 0.0, packed)
        low = pltpu.roll(jnp.where(strict, packed, 0.0), half, 1)
        sides = jnp.concatenate([top, low], axis=0)
        on_diag = jnp.where(jnp.logical_and(left, lane == row), packed, 0.0)
        top_diag = jnp.where(row == lane, total[half : half + 1], 0.0)
        diag = jnp.concatenate([top_diag, pltpu.roll(on_diag, half, 1)], axis=0)
        eye = (iota((members, members), 0) == iota((members, members), 1)).astype(F32)
        system = sides + sides.T + diag + (members - 1.0) * eye
        scale = jnp.sum(jnp.sum(system * eye, axis=1, keepdims=True), axis=0, keepdims=True)
        upper_iter = system / scale
        middle = 1.5 * eye - 0.5 * upper_iter
        upper_iter = exact(upper_iter, middle)
        lower_iter = middle
        for step in range(SWEEPS - 1):
            middle = 1.5 * eye - 0.5 * exact(lower_iter, upper_iter)
            if step < SWEEPS - 2:
                upper_iter = exact(upper_iter, middle)
            lower_iter = exact(middle, lower_iter)
        inv_root = lower_iter * lax.rsqrt(scale)
        proj = jnp.broadcast_to(total[half + 1 : half + 2], (8, members))
        shift = exact(exact(proj, inv_root, NT), inv_root, NT)[:1]
        spread = shift + math.sqrt(members - 1.0) * inv_root
        hold_ref[...] = spread - jnp.mean(spread, axis=1, keepdims=True) + 1.0 / members
        mine = hold_ref[pl.ds(pl.multiple_of(id_ref[1] * local, local), local), :]
        cols_ref[...] = mine.astype(BF)
        flipped = mine.T
        blocks = jnp.concatenate(
            [flipped[m * local : (m + 1) * local] for m in range(count)], axis=1
        ).astype(BF)
        for p in range(npatch):
            out_ref[p] = blocks

    return pl.pallas_call(
        kernel,
        out_shape=(
            jax.ShapeDtypeStruct((local, members), BF),
            jax.ShapeDtypeStruct((npatch, local, members), BF),
        ),
        in_specs=[SMEM, SMEM] + [VMEM] * (1 + len(near)),
        out_specs=(VMEM, VMEM),
        scratch_shapes=[pltpu.VMEM((members, members), F32)],
        compiler_params=params(16),
        name="settle",
    )(listed, ids, own, *near)


def analysis(
    atmos,
    land,
    land_mask,
    tile_owner,
    tile_column,
    tile_weight,
    obs_value,
    observation_column,
    obs_error,
    loc_blocks,
):
    barrier = lax.optimization_barrier
    npatch = lax.axis_size("patch")
    mem_count = lax.axis_size("mem")
    local, levels, columns = atmos.shape
    layers, tiles = (land.shape[1], land.shape[2])
    bucket = 2 * tiles // npatch
    row_width = max(2, npatch // 8)
    mem_rank = lax.axis_index("mem")
    ids = jnp.stack([lax.axis_index("patch"), mem_rank]).astype(I32)

    atmos_rows = atmos.reshape(local * levels, columns)
    atmos_parts = [shifted(atmos_rows, "mem", s) for s in (1, -1, 2)]

    owners = tile_owner.reshape(1, tiles)
    land_rows = land.reshape(local * layers, tiles)
    mask_row = land_mask.reshape(1, tiles)
    ranks, pos, starts = order_tiles(owners, npatch)
    packed = bucket_tiles(
        land_rows,
        layers,
        tile_weight.reshape(tiles // 128, 128),
        land_mask.reshape(tiles // 128, 128),
        owners,
        ranks,
        tile_column.reshape(1, tiles),
        npatch,
        bucket,
    )
    received = lax.all_to_all(packed, "patch", split_axis=0, concat_axis=0, tiled=True)

    early = (tiles // PARTS, 3 * tiles // (2 * PARTS))
    first = sort_land(pos, land_rows, layers, 0, early[0])
    first_prev = shifted(first, "mem", 1)
    first_next = shifted(first, "mem", -1)
    second = sort_land(pos, land_rows, layers, *early)
    second_prev = shifted(second, "mem", 1)
    second_next = shifted(second, "mem", -1)
    rest = sort_land(pos, land_rows, layers, early[1], tiles)

    forecast = screen_forecast(
        received, atmos_rows, levels, observation_column.reshape(-1, 1), mem_count
    )
    forecast, first_prev, first_next, second_prev, second_next, rest = barrier(
        (forecast, first_prev, first_next, second_prev, second_next, rest)
    )
    ensemble = lax.all_to_all(forecast, "mem", split_axis=0, concat_axis=0, tiled=True)
    rest_prev = shifted(rest, "mem", 1)
    rest_next = shifted(rest, "mem", -1)
    first_far = shifted(first_next, "mem", -1)
    second_far = shifted(second_prev, "mem", 1)

    own_stats = screen_stats(ensemble, obs_value.reshape(1, -1), obs_error.reshape(1, -1))
    gaps = (1, -1, row_width, -row_width)
    near = [swapped(own_stats, gap, npatch) for gap in gaps]
    own_cols, mixes = settle(own_stats, near, loc_blocks, ids, gaps, local, npatch)
    own_cols, rest_prev, rest_next = barrier((own_cols, rest_prev, rest_next))
    half = rest.shape[0] // 2
    rest_far = [shifted(rest_prev[:half], "mem", 1), shifted(rest_next[half:], "mem", -1)]
    all_mixes = lax.all_to_all(mixes, "patch", split_axis=0, concat_axis=0, tiled=True)

    slot_source = [mem_rank, mem_rank - 1, mem_rank + 1, mem_rank - 2]
    atmos_out = 0.0
    for part, source in zip([atmos_rows] + atmos_parts, slot_source):
        rows = lax.dynamic_slice_in_dim(own_cols, (source % mem_count) * local, local, 1)
        atmos_out = atmos_out + jnp.einsum(
            "jk,klc->jlc", rows, part.reshape(local, levels, columns), preferred_element_type=F32
        )
    atmos_analysis = atmos_out.astype(BF)

    land_out = mix_land(
        [
            [first, second, rest],
            [first_prev, second_prev, rest_prev],
            [first_next, second_next, rest_next],
            [first_far, second_far] + rest_far,
        ],
        ids,
        starts,
        all_mixes,
        pos,
        land_rows,
        mask_row,
        layers,
    )
    return (atmos_analysis, land_out.reshape(local, layers, tiles))


def solution(mesh):
    in_specs = (
        P("mem", None, "patch"),
        P("mem", None, "patch"),
        P("patch"),
        P("patch", None),
        P("patch"),
        P("patch"),
        P("patch"),
        P("patch"),
        P("patch"),
        P("patch", None),
    )
    out_specs = (P("mem", None, "patch"), P("mem", None, "patch"))
    return jax.shard_map(
        analysis, mesh=mesh, in_specs=in_specs, out_specs=out_specs, check_vma=False
    )
```

```python
import math

import jax
import jax.numpy as jnp
from jax import lax
from jax.experimental import pallas as pl
from jax.experimental.pallas import tpu as pltpu
from jax.sharding import PartitionSpec as P

SWEEPS = 10
PRECISE = lax.Precision.HIGHEST
BF = jnp.bfloat16
F32 = jnp.float32
I32 = jnp.int32

NN = (((1,), (0,)), ((), ()))
NT = (((1,), (1,)), ((), ()))


def dot(a, b, dims=NN):
    return lax.dot_general(a, b, dims, preferred_element_type=F32)


def iota(shape, axis):
    return lax.broadcasted_iota(I32, shape, axis)


VMEM = pl.BlockSpec(memory_space=pltpu.VMEM)
SMEM = pl.BlockSpec(memory_space=pltpu.SMEM)


def params(mib):
    return pltpu.CompilerParams(vmem_limit_bytes=mib * 1024 * 1024)


def shifted(value, axis, steps):
    count = lax.axis_size(axis)
    pairs = [(source, (source + steps) % count) for source in range(count)]
    return lax.ppermute(value, axis, pairs)


PARTS = 4
UNROLL = 4


def partner(patch, gap, npatch):
    return (patch + gap - 2 * gap * ((patch // abs(gap)) % 2) + npatch) % npatch


def swapped(value, gap, npatch):
    pairs = [(source, partner(source, gap, npatch)) for source in range(npatch)]
    return lax.ppermute(value, "patch", pairs)


def order_tiles(owners, npatch):
    tiles = owners.shape[1]
    block = 512
    per_part = tiles // PARTS // block

    def kernel(owner_ref, rank_ref, pos_ref, start_ref):
        before = (iota((block, block), 0) < iota((block, block), 1)).astype(BF)
        lower = (iota((npatch, npatch), 0) > iota((npatch, npatch), 1)).astype(BF)
        done = jnp.zeros((npatch, 1), F32)
        for part in range(PARTS):
            carry = jnp.zeros((npatch, 1), F32)
            held = []
            for c in range(per_part):
                at = (part * per_part + c) * block
                hot = owner_ref[:, at : at + block] == iota((npatch, block), 0)
                ahead = dot(hot.astype(BF), before) + carry
                hot = hot.astype(F32)
                carry = carry + jnp.sum(hot, axis=1, keepdims=True)
                held.append((at, hot, ahead))
            starts = dot(lower, jnp.broadcast_to(carry, (npatch, 128)).astype(BF))[:, :1]
            start_ref[:, part : part + 1] = starts.astype(I32)
            for at, hot, ahead in held:
                rank = jnp.sum(hot * (ahead + done), axis=0, keepdims=True)
                pos = jnp.sum(hot * (ahead + starts), axis=0, keepdims=True)
                rank_ref[:, at : at + block] = rank.astype(I32)
                pos_ref[:, at : at + block] = pos.astype(I32)
            done = done + carry
        start_ref[:, PARTS:] = jnp.zeros((npatch, PARTS), I32)

    return pl.pallas_call(
        kernel,
        out_shape=(
            jax.ShapeDtypeStruct((1, tiles), I32),
            jax.ShapeDtypeStruct((1, tiles), I32),
            jax.ShapeDtypeStruct((npatch, 2 * PARTS), I32),
        ),
        in_specs=[VMEM],
        out_specs=(VMEM, VMEM, VMEM),
        compiler_params=params(60),
        name="order_tiles",
    )(owners)


def bucket_tiles(land_rows, levels, weight, mask, owners, ranks, columns, npatch, bucket):
    width, tiles = land_rows.shape
    rows = width // levels
    low = 4
    high = npatch // low
    block = 1024
    steps = tiles // block

    def kernel(
        x_ref,
        weight_ref,
        mask_ref,
        owner_ref,
        rank_ref,
        col_ref,
        out_ref,
        acc_ref,
        cacc_ref,
        keep_ref,
    ):
        step = pl.program_id(0)
        owner = owner_ref[...]
        slot = (owner & (low - 1)) * bucket + rank_ref[...]
        hot = (iota((low * bucket, block), 0) == slot).astype(F32).astype(BF)
        group = owner >> 2
        surface = (iota((rows, width), 0) * levels == iota((rows, width), 1)).astype(F32)

        @pl.when(step == 0)
        def _():
            keep_ref[...] = weight_ref[...].astype(F32) * mask_ref[...].astype(F32)

        per_step = block // 128
        keep = keep_ref[pl.ds(pl.multiple_of(step * per_step, per_step), per_step), :]
        keep = jnp.concatenate([keep[c : c + 1] for c in range(per_step)], axis=1)
        value = (dot(surface.astype(BF), x_ref[...]) * keep).astype(BF)
        zero = jnp.zeros_like(value)
        picked = jnp.concatenate(
            [jnp.where(group == g, value, zero) for g in range(high)], axis=0
        )
        part = dot(picked, hot, NT)
        col = col_ref[...]
        half = iota((2 * high, block), 0)
        digit = jnp.where((half & 1) == 0, col >> 5, col & 31)
        digits = jnp.where((half >> 1) == group, digit, 0).astype(F32).astype(BF)
        cpart = dot(digits, hot, NT)

        @pl.when(step == 0)
        def _():
            acc_ref[...] = part
            cacc_ref[...] = cpart

        @pl.when(step > 0)
        def _():
            acc_ref[...] += part
            cacc_ref[...] += cpart

        @pl.when(step == steps - 1)
        def _():
            for o in range(npatch):
                g, b = o // low, o % low
                cut = slice(b * bucket, (b + 1) * bucket)
                out_ref[o, :rows, :] = acc_ref[g * rows : (g + 1) * rows, cut].astype(BF)
                out_ref[o, rows : rows + 2, :] = cacc_ref[2 * g : 2 * g + 2, cut].astype(BF)

    lane = pl.BlockSpec((1, block), lambda i: (0, i))
    return pl.pallas_call(
        kernel,
        grid=(steps,),
        out_shape=jax.ShapeDtypeStruct((npatch, rows + 2, bucket), BF),
        in_specs=[pl.BlockSpec((width, block), lambda i: (0, i)), VMEM, VMEM] + [lane] * 3,
        out_specs=pl.BlockSpec((npatch, rows + 2, bucket), lambda i: (0, 0, 0)),
        scratch_shapes=[
            pltpu.VMEM((high * rows, low * bucket), F32),
            pltpu.VMEM((2 * high, low * bucket), F32),
            pltpu.VMEM((tiles // 128, 128), F32),
        ],
        compiler_params=params(60),
        name="bucket_tiles",
    )(land_rows, weight, mask, owners, ranks, columns)


def lane_swap(rows, a, b):
    source = iota((rows, rows), 0)
    target = iota((rows, rows), 1)
    return ((source % b) * a + source // b == target).astype(F32).astype(BF)


def sort_land(pos, land_rows, levels, *cuts):
    width, tiles = land_rows.shape
    span = tiles // PARTS
    block = 512
    begin, end = cuts[0], cuts[-1]
    one = begin // span == (end - 1) // span
    taken = span if one else tiles
    shift = begin // span * span if one else 0
    sizes = [b - a for a, b in zip(cuts, cuts[1:])]

    def kernel(pos_ref, x_ref, *out_refs):
        swap = lane_swap(width, width // levels, levels)
        for out_ref, first, last in zip(out_refs, cuts, cuts[1:]):
            for at in range(first, last, block):
                part = at // span * span
                cut = slice(part - shift, part - shift + span)
                place = iota((block, span), 0) + (at - part)
                hot = (place == pos_ref[:, cut]).astype(F32).astype(BF)
                moved = dot(hot, x_ref[:, cut], NT).astype(BF)
                out_ref[at - first : at - first + block, :] = dot(moved, swap).astype(BF)

    return pl.pallas_call(
        kernel,
        grid=(1,),
        out_shape=[jax.ShapeDtypeStruct((size, width), BF) for size in sizes],
        in_specs=[
            pl.BlockSpec((1, taken), lambda i: (0, shift // taken)),
            pl.BlockSpec((width, taken), lambda i: (0, shift // taken)),
        ],
        out_specs=[pl.BlockSpec((size, width), lambda i: (0, 0)) for size in sizes],
        compiler_params=params(60),
        name="sort_land",
    )(pos, land_rows)


def screen_forecast(received, base_rows, levels, obs_column, copies):
    npatch, rows2, _ = received.shape
    rows = rows2 - 2
    nobs = obs_column.shape[0]
    width, columns = base_rows.shape
    group = 8

    def kernel(in_ref, base_ref, obs_ref, out_ref):
        obs = obs_ref[...]
        place = iota((nobs, columns), 1)
        surface = (iota((rows, width), 0) * levels == iota((rows, width), 1)).astype(F32)
        base = dot(surface.astype(BF), base_ref[...]).astype(BF)
        acc = dot(base, (obs == place).astype(F32).astype(BF), NT)
        for g in range(npatch // group):
            values = jnp.concatenate(
                [in_ref[g * group + i, :rows, :] for i in range(group)], axis=1
            )
            digits = jnp.concatenate(
                [in_ref[g * group + i, rows:, :] for i in range(group)], axis=1
            ).astype(F32)
            col = (digits[0:1] * 32.0 + digits[1:2]).astype(I32)
            acc = acc + dot(values, (obs == col).astype(F32).astype(BF), NT)
        value = acc.astype(BF)
        for m in range(copies):
            out_ref[m] = value

    return pl.pallas_call(
        kernel,
        out_shape=jax.ShapeDtypeStruct((copies, rows, nobs), BF),
        in_specs=[VMEM, VMEM, VMEM],
        out_specs=VMEM,
        compiler_params=params(24),
        name="screen_forecast",
    )(received, base_rows, obs_column)


def mix_land(pieces, ids, starts, mixes, pos, land_rows, mask_row, levels):
    slots = len(pieces)
    flat = [piece for group in pieces for piece in group]
    places = [
        (s, sum(p.shape[0] for p in group[:i]))
        for s, group in enumerate(pieces)
        for i in range(len(group))
    ]
    width, tiles = land_rows.shape
    local = width // levels
    npatch = mixes.shape[0]
    members = mixes.shape[2]
    span = tiles // PARTS
    window = 48
    lanes = 128
    count = len(flat)

    def kernel(id_ref, start_ref, *refs):
        piece_refs = refs[:count]
        mix_ref, pos_ref, land_ref, mask_ref, out_ref = refs[count : count + 5]
        state_ref, tiled_ref, y_ref, sems = refs[count + 5 :]
        step = pl.program_id(0)

        @pl.when(step == 0)
        def _():
            copies = [
                pltpu.make_async_copy(
                    piece_refs[i],
                    state_ref.at[s, pl.ds(at, piece_refs[i].shape[0]), :],
                    sems.at[i],
                )
                for i, (s, at) in enumerate(places)
            ]
            for copy in copies:
                copy.start()
            for s in range(slots):
                spread = (
                    iota((members, lanes), 0)
                    == (iota((members, lanes), 1) & (local - 1)) + (id_ref[1] + (0, slots - 1, 1, 2)[s]) % slots * local
                )
                tiled_ref[:, s * lanes : (s + 1) * lanes] = dot(
                    mix_ref[...], spread.astype(F32).astype(BF)
                ).astype(BF)
            lane_level = iota((local, lanes), 1) // local
            for copy in copies:
                copy.wait()

            def weight_of(o, s):
                at = pl.multiple_of(o * local, local)
                parts = []
                for t in (s, s + 1):
                    small = tiled_ref[pl.ds(at, local), t * lanes : (t + 1) * lanes]
                    zero = jnp.zeros_like(small)
                    parts += [
                        jnp.where(lane_level == l, small, zero) for l in range(lanes // local)
                    ]
                return jnp.concatenate(parts, axis=0)

            def mixed(o, cuts):
                acc = None
                for s in range(0, slots, 2):
                    rows = [
                        jnp.concatenate(
                            [
                                state_ref[t, pl.ds(at, window), h * lanes : (h + 1) * lanes]
                                for t in (s, s + 1)
                            ],
                            axis=1,
                        )
                        for h in range(width // lanes)
                        for at in cuts
                    ]
                    part = dot(jnp.concatenate(rows, axis=0), weight_of(o, s))
                    acc = part if acc is None else acc + part
                half = len(cuts) * window
                return jnp.concatenate(
                    [acc[h * half : (h + 1) * half] for h in range(width // lanes)], axis=1
                ).astype(BF)

            def put(part, base, first, end, value):
                at = pl.multiple_of(part * span + base, 16)
                row = iota((window, width), 0) + base
                keep = row >= first
                if end is not None:
                    keep = jnp.logical_and(keep, row < end)
                old = y_ref[pl.ds(at, window), :]
                y_ref[pl.ds(at, window), :] = jnp.where(keep, value, old)

            def begin(first):
                return pl.multiple_of(jnp.minimum((first // 16) * 16, span - window), 16)

            def bounds(o):
                firsts = [start_ref[o, q] for q in range(PARTS)]
                after = jnp.minimum(o + 1, npatch - 1)
                ends = [
                    jnp.where(o == npatch - 1, span, start_ref[after, q]) for q in range(PARTS)
                ]
                return firsts, ends, [begin(first) for first in firsts]

            def owners(i, unused):
                group = [i * UNROLL + u for u in range(UNROLL)]
                limits = [bounds(o) for o in group]
                values = [
                    mixed(o, [pl.multiple_of(q * span + bases[q], 16) for q in range(PARTS)])
                    for o, (firsts, ends, bases) in zip(group, limits)
                ]
                for value, (firsts, ends, bases) in zip(values, limits):
                    for q in range(PARTS):
                        put(q, bases[q], firsts[q], None, value[q * window : (q + 1) * window])
                most = 0
                for firsts, ends, bases in limits:
                    for q in range(PARTS):
                        most = jnp.maximum(most, ends[q] - bases[q] - window)

                @pl.when(most > 0)
                def _():
                    for o, (firsts, ends, bases) in zip(group, limits):
                        lacks = [
                            jnp.maximum(ends[q] - bases[q] - window, 0) for q in range(PARTS)
                        ]

                        @pl.when(lacks[0] + lacks[1] + lacks[2] + lacks[3] > 0)
                        def _():
                            for q in range(PARTS):

                                def more(n, unused, q=q):
                                    base = begin(bases[q] + (n + 1) * window)
                                    at = pl.multiple_of(q * span + base, 16)
                                    put(q, base, firsts[q], ends[q], mixed(o, [at]))
                                    return unused

                                lax.fori_loop(0, (lacks[q] + window - 1) // window, more, 0)

                return unused

            lax.fori_loop(0, npatch // UNROLL, owners, 0)

        hot = (iota((span, span), 0) == pos_ref[...]).astype(F32).astype(BF)
        rows = y_ref[pl.ds(pl.multiple_of(step * span, span), span), :]
        turned = dot(lane_swap(width, local, levels), rows, NT).astype(BF)
        back = dot(turned, hot).astype(BF)
        out_ref[...] = jnp.where(mask_ref[...] == 1, back, land_ref[...])

    return pl.pallas_call(
        kernel,
        grid=(PARTS,),
        out_shape=jax.ShapeDtypeStruct((width, tiles), BF),
        in_specs=[SMEM, SMEM]
        + [pl.BlockSpec(memory_space=pl.ANY)] * count
        + [
            VMEM,
            pl.BlockSpec((1, span), lambda i: (0, i)),
            pl.BlockSpec((width, span), lambda i: (0, i)),
            pl.BlockSpec((1, span), lambda i: (0, i)),
        ],
        out_specs=pl.BlockSpec((width, span), lambda i: (0, i)),
        scratch_shapes=[
            pltpu.VMEM((slots, tiles, width), BF),
            pltpu.VMEM((npatch * local, slots * lanes), BF),
            pltpu.VMEM((tiles, width), BF),
            pltpu.SemaphoreType.DMA((count,)),
        ],
        compiler_params=params(60),
        name="mix_land",
    )(
        ids,
        starts,
        *flat,
        mixes.reshape(npatch * local, members),
        pos,
        land_rows,
        mask_row,
    )


def exact(a, b, dims=NN):
    return lax.dot_general(a, b, dims, precision=PRECISE, preferred_element_type=F32)


def screen_stats(ensemble, obs_value, obs_error):
    count, local, nobs = ensemble.shape
    members = count * local
    half = members // 2

    def kernel(in_ref, value_ref, error_ref, out_ref):
        rows = jnp.concatenate([in_ref[m].astype(F32) for m in range(count)], axis=0)
        center = jnp.mean(rows, axis=0, keepdims=True)
        inverse_sd = lax.rsqrt(error_ref[...])
        scaled = (rows - center) * inverse_sd
        innovation = (value_ref[...] - center) * inverse_sd
        gram = exact(scaled, scaled, NT)
        proj = exact(jnp.broadcast_to(innovation, (8, nobs)), scaled, NT)
        row, lane = iota((half, members), 0), iota((half, members), 1)
        top = gram[:half]
        from_low = jnp.logical_and(lane < half, lane >= row)
        out_ref[:half, :] = jnp.where(from_low, pltpu.roll(gram[half:], half, 1), top)
        diag = jnp.sum(jnp.where(row == lane, top, 0.0), axis=0, keepdims=True)
        tail = iota((8, members), 0)
        out_ref[half:, :] = jnp.where(tail == 0, diag, jnp.where(tail == 1, proj, 0.0))

    return pl.pallas_call(
        kernel,
        out_shape=jax.ShapeDtypeStruct((half + 8, members), F32),
        in_specs=[VMEM, VMEM, VMEM],
        out_specs=VMEM,
        compiler_params=params(16),
        name="screen_stats",
    )(ensemble, obs_value, obs_error)


def settle(own, near, listed, ids, gaps, local, npatch):
    members = own.shape[1]
    half = members // 2
    count = members // local
    names = listed.shape[1]

    def kernel(list_ref, id_ref, own_ref, *refs):
        near_refs = refs[: len(near)]
        cols_ref, out_ref, hold_ref = refs[len(near) :]
        total = own_ref[...]
        for d in range(len(near)):
            source = partner(id_ref[0], gaps[d], npatch)
            used = 0
            for i in range(names):
                used = used + jnp.where(list_ref[0, i] == source, 1, 0)
            total = total + used.astype(F32) * near_refs[d][...]
        packed = total[:half]
        row, lane = iota((half, members), 0), iota((half, members), 1)
        left = lane < half
        upper = jnp.logical_and(left, lane >= row)
        strict = jnp.logical_and(left, lane > row)
        top = jnp.where(upper, 0.0, packed)
        low = pltpu.roll(jnp.where(strict, packed, 0.0), half, 1)
        sides = jnp.concatenate([top, low], axis=0)
        on_diag = jnp.where(jnp.logical_and(left, lane == row), packed, 0.0)
        top_diag = jnp.where(row == lane, total[half : half + 1], 0.0)
        diag = jnp.concatenate([top_diag, pltpu.roll(on_diag, half, 1)], axis=0)
        eye = (iota((members, members), 0) == iota((members, members), 1)).astype(F32)
        system = sides + sides.T + diag + (members - 1.0) * eye
        scale = jnp.sum(jnp.sum(system * eye, axis=1, keepdims=True), axis=0, keepdims=True)
        upper_iter = system / scale
        middle = 1.5 * eye - 0.5 * upper_iter
        upper_iter = exact(upper_iter, middle)
        lower_iter = middle
        for step in range(SWEEPS - 1):
            middle = 1.5 * eye - 0.5 * exact(lower_iter, upper_iter)
            if step < SWEEPS - 2:
                upper_iter = exact(upper_iter, middle)
            lower_iter = exact(middle, lower_iter)
        inv_root = lower_iter * lax.rsqrt(scale)
        proj = jnp.broadcast_to(total[half + 1 : half + 2], (8, members))
        shift = exact(exact(proj, inv_root, NT), inv_root, NT)[:1]
        spread = shift + math.sqrt(members - 1.0) * inv_root
        hold_ref[...] = spread - jnp.mean(spread, axis=1, keepdims=True) + 1.0 / members
        mine = hold_ref[pl.ds(pl.multiple_of(id_ref[1] * local, local), local), :]
        cols_ref[...] = mine.astype(BF)
        flipped = mine.T
        blocks = jnp.concatenate(
            [flipped[m * local : (m + 1) * local] for m in range(count)], axis=1
        ).astype(BF)
        for p in range(npatch):
            out_ref[p] = blocks

    return pl.pallas_call(
        kernel,
        out_shape=(
            jax.ShapeDtypeStruct((local, members), BF),
            jax.ShapeDtypeStruct((npatch, local, members), BF),
        ),
        in_specs=[SMEM, SMEM] + [VMEM] * (1 + len(near)),
        out_specs=(VMEM, VMEM),
        scratch_shapes=[pltpu.VMEM((members, members), F32)],
        compiler_params=params(16),
        name="settle",
    )(listed, ids, own, *near)


def repeat(value):
    def kernel(in_ref, out_ref):
        out_ref[...] = in_ref[...]

    return pl.pallas_call(
        kernel,
        out_shape=jax.ShapeDtypeStruct(value.shape, value.dtype),
        in_specs=[VMEM],
        out_specs=VMEM,
        compiler_params=params(1),
        name="repeat",
    )(value)


def analysis(
    atmos,
    land,
    land_mask,
    tile_owner,
    tile_column,
    tile_weight,
    obs_value,
    observation_column,
    obs_error,
    loc_blocks,
):
    barrier = lax.optimization_barrier
    npatch = lax.axis_size("patch")
    mem_count = lax.axis_size("mem")
    local, levels, columns = atmos.shape
    layers, tiles = (land.shape[1], land.shape[2])
    bucket = 2 * tiles // npatch
    row_width = max(2, npatch // 8)
    mem_rank = lax.axis_index("mem")
    ids = jnp.stack([lax.axis_index("patch"), mem_rank]).astype(I32)

    atmos_rows = atmos.reshape(local * levels, columns)
    atmos_parts = [shifted(atmos_rows, "mem", s) for s in (1, -1, 2)]

    owners = tile_owner.reshape(1, tiles)
    land_rows = land.reshape(local * layers, tiles)
    mask_row = land_mask.reshape(1, tiles)
    ranks, pos, starts = order_tiles(owners, npatch)
    packed = bucket_tiles(
        land_rows,
        layers,
        tile_weight.reshape(tiles // 128, 128),
        land_mask.reshape(tiles // 128, 128),
        owners,
        ranks,
        tile_column.reshape(1, tiles),
        npatch,
        bucket,
    )
    received = lax.all_to_all(packed, "patch", split_axis=0, concat_axis=0, tiled=True)

    early = (tiles // PARTS, 3 * tiles // (2 * PARTS))
    late = 3 * tiles // PARTS
    (first,) = sort_land(pos, land_rows, layers, 0, early[0])
    first_prev = shifted(first, "mem", 1)
    first_next = shifted(first, "mem", -1)
    (second,) = sort_land(pos, land_rows, layers, *early)
    second_prev = shifted(second, "mem", 1)
    second_next = shifted(second, "mem", -1)
    third, fourth = sort_land(pos, land_rows, layers, early[1], late, tiles)

    forecast = screen_forecast(
        received, atmos_rows, levels, observation_column.reshape(-1, 1), mem_count
    )
    forecast, first_prev, first_next, second_prev, second_next, third, fourth = barrier(
        (forecast, first_prev, first_next, second_prev, second_next, third, fourth)
    )
    ensemble = lax.all_to_all(forecast, "mem", split_axis=0, concat_axis=0, tiled=True)
    third_prev = shifted(third, "mem", 1)
    third_next = shifted(third, "mem", -1)
    fourth_prev = shifted(fourth, "mem", 1)
    fourth_next = shifted(fourth, "mem", -1)
    first_far = shifted(first_next, "mem", -1)
    second_far = shifted(second_prev, "mem", 1)
    third_far = shifted(third_prev, "mem", 1)

    own_stats = screen_stats(ensemble, obs_value.reshape(1, -1), obs_error.reshape(1, -1))
    gaps = (1, -1, row_width, -row_width)
    near = [swapped(own_stats, gap, npatch) for gap in gaps]
    own_cols, mixes = settle(own_stats, near, loc_blocks, ids, gaps, local, npatch)
    own_cols = repeat(own_cols)
    fourth_far = shifted(fourth_next, "mem", -1)
    all_mixes = lax.all_to_all(mixes, "patch", split_axis=0, concat_axis=0, tiled=True)

    slot_source = [mem_rank, mem_rank - 1, mem_rank + 1, mem_rank - 2]
    atmos_out = 0.0
    for part, source in zip([atmos_rows] + atmos_parts, slot_source):
        rows = lax.dynamic_slice_in_dim(own_cols, (source % mem_count) * local, local, 1)
        atmos_out = atmos_out + jnp.einsum(
            "jk,klc->jlc", rows, part.reshape(local, levels, columns), preferred_element_type=F32
        )
    atmos_analysis = atmos_out.astype(BF)

    land_out = mix_land(
        [
            [first, second, third, fourth],
            [first_prev, second_prev, third_prev, fourth_prev],
            [first_next, second_next, third_next, fourth_next],
            [first_far, second_far, third_far, fourth_far],
        ],
        ids,
        starts,
        all_mixes,
        pos,
        land_rows,
        mask_row,
        layers,
    )
    return (atmos_analysis, land_out.reshape(local, layers, tiles))


def solution(mesh):
    in_specs = (
        P("mem", None, "patch"),
        P("mem", None, "patch"),
        P("patch"),
        P("patch", None),
        P("patch"),
        P("patch"),
        P("patch"),
        P("patch"),
        P("patch"),
        P("patch", None),
    )
    out_specs = (P("mem", None, "patch"), P("mem", None, "patch"))
    return jax.shard_map(
        analysis, mesh=mesh, in_specs=in_specs, out_specs=out_specs, check_vma=False
    )
```
